256 devices in a mesh: ex: 4 (over x), row: 8 (over y, core), col: 8 (over z).
Axes of the slice: x: 4, y: 4, z: 8, core: 2. Of those that a mesh axis runs over, the one named last changes fastest.
Arguments:
- inputs: bfloat16 [32, 256, 256, 128], P('ex', 'row', 'col'), may hold values from -6 to 6
- cotangent: bfloat16 [32, 256, 256, 128], P('ex', 'row', 'col'), may hold values from -200 to 200, as said below
- weight: bfloat16 [3, 3, 128, 128], replicated, may hold values from -0.1875 to 0.1875
- bias: float32 [128], replicated, may hold values from -1 to 1
- noise_weight: float32 [1152, 128], P(('row', 'col')), may hold values from -6 to 6
- noise_bias: float32 [128], replicated, may hold values from -6 to 6
Outputs:
- input_grad: bfloat16 [32, 256, 256, 128], P('ex', 'row', 'col')
- grad_weight: float32 [1152, 128], P(('row', 'col'))
- grad_bias: float32 [128], replicated
The draws below stay inside these ranges and needn't reach their ends.
Inputs may be any that keep to these rules, and one draw needn't show every extreme that they name: Each example's cotangent has its own overall scale.
All inputs are finite; a program needn't handle non-finite values.
Results may differ from the reference program's by a relative error of at most 0.0055.
Values may be sent and summed in bfloat16 or wider, within the bound.
A program may use at most 64 MiB of HBM per device.

```python
import math
import jax
import jax.numpy as jnp
from jax import lax

CHANNELS = 128
HEIGHT = 256
WIDTH = 256
BATCH = 32


def draw_cotangent(key, part):
    key_order, key_jitter, key_base = jax.random.split(jax.random.fold_in(key, 71), 3)
    order = jax.random.permutation(key_order, BATCH).astype(jnp.float32)
    jitter = jax.random.uniform(key_jitter, (BATCH,), jnp.float32)
    scales = 0.2 * 25.0 ** ((order + jitter) / BATCH)
    row_pos = jnp.arange(HEIGHT, dtype=jnp.float32) / HEIGHT
    col_pos = jnp.arange(WIDTH, dtype=jnp.float32) / WIDTH
    spatial = (3.0 ** row_pos)[:, None] * (3.0 ** col_pos)[None, :]
    shape = (BATCH, HEIGHT, WIDTH, CHANNELS)
    base = jax.random.truncated_normal(key_base, -4.0, 4.0, shape, jnp.float32)
    values = base * scales[:, None, None, None] * spatial[None, :, :, None]
    return values.astype(jnp.bfloat16)


def shard_levels(stream_key, shape, shards, least, high):
    def one(dim, parts):
        draws = jax.random.uniform(jax.random.fold_in(jax.random.fold_in(stream_key, 6), dim), (parts,), jnp.float32, least / len(shards), high / len(shards))
        return jnp.repeat(jnp.exp(draws), shape[dim] // parts).reshape((-1,) + (1,) * (len(shape) - dim - 1))

    gain = one(*shards[0])
    for cut in shards[1:]:
        gain = gain * one(*cut)
    return gain


def centred(own_key, extent, scale, reach, cuts=(), held_as=jnp.bfloat16):
    array = scale * jax.random.normal(own_key, extent, jnp.float32)
    if cuts:
        array = array * shard_levels(own_key, extent, cuts, -0.22, 0.18)
    return jnp.clip(array, -reach, reach).astype(held_as)


def setup_inputs(seed: int = 0) -> dict:
    key_list = jax.random.split(jax.random.key(seed), 7)
    inputs = centred(key_list[0], (BATCH, HEIGHT, WIDTH, CHANNELS), 1.0, 6.0, ((0, 4), (1, 8), (2, 8)))
    cotangent = draw_cotangent(jax.random.fold_in(key_list[6], 71), 0)
    weight = centred(key_list[2], (3, 3, CHANNELS, CHANNELS), (9 * CHANNELS) ** -0.5, 0.1875)
    bias = jnp.clip(jax.random.uniform(key_list[3], (CHANNELS,), jnp.float32, -1.0, 1.0), -1.0, 1.0)
    noise_weight = centred(key_list[4], (9 * CHANNELS, CHANNELS), 1.0, 6.0, ((0, 64),), jnp.float32)
    noise_bias = centred(key_list[5], (CHANNELS,), 1.0, 6.0, (), jnp.float32)
    return {"inputs": inputs, "cotangent": cotangent, "weight": weight, "bias": bias, "noise_weight": noise_weight, "noise_bias": noise_bias}


noise_multiplier = 0.002
epsilon = 1e-06

def example_grads(example_in, example_cot, weight, bias):
    padded = jnp.pad(example_in, ((1, 1), (1, 1), (0, 0)))
    preact = bias
    for tap_row in range(3):
        for tap_col in range(3):
            window = padded[tap_row:tap_row + HEIGHT, tap_col:tap_col + WIDTH].reshape(-1, CHANNELS)
            preact = preact + jnp.dot(window, weight[tap_row, tap_col], preferred_element_type=jnp.float32)
    sigmoid_z = jax.nn.sigmoid(preact)
    slope = sigmoid_z * (1.0 + preact * (1.0 - sigmoid_z))
    grad_z = (example_cot.reshape(-1, CHANNELS).astype(jnp.float32) * slope).astype(jnp.bfloat16)
    grad_pad = jnp.pad(grad_z.reshape(HEIGHT, WIDTH, CHANNELS), ((1, 1), (1, 1), (0, 0)))
    backward = jnp.zeros((HEIGHT * WIDTH, CHANNELS), jnp.float32)
    pieces = []
    for tap_row in range(3):
        for tap_col in range(3):
            shifted = grad_pad[2 - tap_row:2 - tap_row + HEIGHT, 2 - tap_col:2 - tap_col + WIDTH].reshape(-1, CHANNELS)
            backward = backward + jnp.dot(shifted, weight[tap_row, tap_col].T, preferred_element_type=jnp.float32)
            window = padded[tap_row:tap_row + HEIGHT, tap_col:tap_col + WIDTH].reshape(-1, CHANNELS)
            pieces.append(jnp.dot(window.T, grad_z, preferred_element_type=jnp.float32))
    input_grad = backward.astype(jnp.bfloat16).reshape(HEIGHT, WIDTH, CHANNELS)
    per_weight = jnp.stack(pieces).reshape(9 * CHANNELS, CHANNELS)
    per_bias = lax.optimization_barrier(jnp.sum(grad_z.astype(jnp.float32), axis=0))
    return (input_grad, per_weight, per_bias)

def reference(inputs, cotangent, weight, bias, noise_weight, noise_bias):
    clip = math.sqrt(HEIGHT * WIDTH * 9 * CHANNELS * CHANNELS)

    def accumulate(totals, operands):
        input_grad, per_weight, per_bias = example_grads(operands[0], operands[1], weight, bias)
        norm_value = jnp.sqrt(jnp.sum(per_weight * per_weight) + jnp.sum(per_bias * per_bias) + epsilon)
        factor = jnp.minimum(1.0, clip / norm_value)
        return ((totals[0] + factor * per_weight, totals[1] + factor * per_bias), input_grad)
    start = (jnp.zeros((9 * CHANNELS, CHANNELS), jnp.float32), jnp.zeros((CHANNELS,), jnp.float32))
    sums, input_grad = lax.scan(accumulate, start, (inputs, cotangent))
    scale = 1.0 / math.sqrt(BATCH * HEIGHT * WIDTH)
    grad_weight = (sums[0] + noise_multiplier * clip * noise_weight) * scale
    grad_bias = (sums[1] + noise_multiplier * clip * noise_bias) * scale
    return (input_grad, grad_weight, grad_bias)
```

```python
import functools
import math

import jax
import jax.numpy as jnp
from jax import lax
from jax.experimental import pallas as pl
from jax.experimental.pallas import tpu as pltpu
from jax.sharding import PartitionSpec as P

noise_multiplier = 0.002
epsilon = 1e-06
F32 = jnp.float32
BF16 = jnp.bfloat16
N_EX = 8
TILE = 32
CH = 128
PITCH = 48
PIX = TILE * TILE
ROWS = 9 * CH
CHUNK = ROWS // 8
OWN = CHUNK // 8
PIECE = 32


def kernel(
    clip, scale,
    x_hbm, cot_hbm, w_ref, b_ref, nw_ref, nb_ref, xe_ref, xc_ref,
    out_hbm, gw_ref, gb_ref,
    xp, cot, gp, xcol, xcor, gcol, gcor, ge, gc, wide, taps, gt, g32, wback, acc, outb,
    stage, crx, y1own, y1tx, y1rx, y2own, y2tx, y2rx, t32, zst, zrx, zacc, bpart,
    n1st, n1rx, n2st, n2rx, fst, est, erx,
    lx_s, lc_s, lo_s, xh_s, xh_r, gh_s, gh_r, c_s, c_r, y1_s, y1_r, y2_s, y2_r, z_s, z_r,
    n1_s, n1_r, n2_s, n2_r, e_s, e_r,
):
    e, r, c = lax.axis_index("ex"), lax.axis_index("row"), lax.axis_index("col")
    core, y = r % 2, r // 2
    up, down, left, right = (r + 7) % 8, (r + 1) % 8, (c + 7) % 8, (c + 1) % 8
    mate = r + 1 - 2 * core
    flip, mirror = y + 1 - 2 * (y % 2), 3 - y
    p1 = flip + core * (mirror - flip)
    p2 = mirror + core * (flip - mirror)
    far = (y + 2) % 4
    corners = ((up, left), (up, right), (down, left), (down, right))

    def remote(src, dst, s_sem, r_sem, to_row, to_col, to_ex=None):
        return pltpu.make_async_remote_copy(
            src_ref=src, dst_ref=dst, send_sem=s_sem, recv_sem=r_sem,
            device_id=(e if to_ex is None else to_ex, to_row, to_col),
            device_id_type=pl.DeviceIdType.MESH,
        )

    def load_x(n):
        return pltpu.make_async_copy(x_hbm.at[n], xp.at[n, 1 : TILE + 1], lx_s.at[n])

    def load_cot(n):
        return pltpu.make_async_copy(cot_hbm.at[n], cot.at[n], lc_s.at[n])

    for n in range(N_EX):
        load_x(n).start()
    for n in range(N_EX):
        load_cot(n).start()

    barrier = pltpu.get_barrier_semaphore()
    partners = list(corners)
    partners += [((r + k) % 8, c) for k in range(1, 8)]
    partners += [(r, (c + k) % 8) for k in range(1, 8)]
    for to_row, to_col in partners:
        pl.semaphore_signal(barrier, inc=1, device_id=(e, to_row, to_col), device_id_type=pl.DeviceIdType.MESH)
    for k in range(1, 4):
        pl.semaphore_signal(barrier, inc=1, device_id=((e + k) % 4, r, c), device_id_type=pl.DeviceIdType.MESH)

    for a in range(3):
        for b in range(3):
            wback[2 - a, (2 - b) * CH : (3 - b) * CH, :] = w_ref[a, b * CH : (b + 1) * CH, :].T
    t32[...] = jnp.zeros_like(t32)
    pl.semaphore_wait(barrier, 21)

    def x_halo():
        copies = [
            remote(x_hbm.at[:, TILE - 1], xp.at[:, 0], xh_s.at[0], xh_r.at[0], down, c),
            remote(x_hbm.at[:, 0], xp.at[:, TILE + 1], xh_s.at[1], xh_r.at[1], up, c),
            remote(xe_ref.at[1], xcol.at[0], xh_s.at[2], xh_r.at[2], r, right),
            remote(xe_ref.at[0], xcol.at[1], xh_s.at[3], xh_r.at[3], r, left),
        ]
        for k, (to_row, to_col) in enumerate(corners):
            copies.append(
                remote(xc_ref.at[k], xcor.at[3 - k], xh_s.at[4 + k], xh_r.at[7 - k], to_row, to_col)
            )
        return copies

    def g_halo(n):
        copies = [
            remote(gp.at[n, TILE], gp.at[n, 0], gh_s.at[0, n], gh_r.at[0, n], down, c),
            remote(gp.at[n, 1], gp.at[n, TILE + 1], gh_s.at[1, n], gh_r.at[1, n], up, c),
            remote(ge.at[1, n], gcol.at[0, n], gh_s.at[2, n], gh_r.at[2, n], r, right),
            remote(ge.at[0, n], gcol.at[1, n], gh_s.at[3, n], gh_r.at[3, n], r, left),
        ]
        for k, (to_row, to_col) in enumerate(corners):
            copies.append(
                remote(gc.at[k, n], gcor.at[3 - k, n], gh_s.at[4 + k, n], gh_r.at[7 - k, n], to_row, to_col)
            )
        return copies

    def clear(pad, col, cor, n):
        count, at = (N_EX, slice(None)) if n is None else (1, pl.ds(n, 1))
        row_zero = jnp.zeros((count, 1, TILE, CH), BF16)
        col_zero = jnp.zeros((1, count, TILE, CH), BF16)
        cor_zero = jnp.zeros((1, count, 16, CH), BF16)

        @pl.when(r == 0)
        def _():
            pad[at, 0:1] = row_zero
            cor[0:1, at] = cor_zero
            cor[1:2, at] = cor_zero

        @pl.when(r == 7)
        def _():
            pad[at, TILE + 1 : TILE + 2] = row_zero
            cor[2:3, at] = cor_zero
            cor[3:4, at] = cor_zero

        @pl.when(c == 0)
        def _():
            col[0:1, at] = col_zero
            cor[0:1, at] = cor_zero
            cor[2:3, at] = cor_zero

        @pl.when(c == 7)
        def _():
            col[1:2, at] = col_zero
            cor[1:2, at] = cor_zero
            cor[3:4, at] = cor_zero

    def spread(pad, col, cor, n):
        tile = wide.reshape(TILE + 2, PITCH, CH)
        tile[:, 8 : 8 + TILE, :] = pad[n].astype(F32)
        for side, slot in ((0, 7), (1, 8 + TILE)):
            wide[pl.ds(PITCH + slot, TILE, stride=PITCH), :] = col[side, n].astype(F32)
            wide[slot : slot + 1, :] = cor[side, n].astype(F32)[0:1]
            last = (TILE + 1) * PITCH + slot
            wide[last : last + 1, :] = cor[2 + side, n].astype(F32)[0:1]
        taps[:, :, CH : 2 * CH] = pad[n]
        taps[:, :, 0:CH] = tile[:, 7 : 7 + TILE, :].astype(BF16)
        taps[:, :, 2 * CH :] = tile[:, 9 : 9 + TILE, :].astype(BF16)

    def conv(weights):
        total = None
        for a in range(3):
            part = jnp.dot(
                taps[a : a + TILE].reshape(PIX, 3 * CH), weights[a], preferred_element_type=F32
            )
            total = part if total is None else total + part
        return total

    def core_copy(m):
        return remote(stage.at[m, 1 - core], crx.at[m], c_s.at[m], c_r.at[m], mate, c)

    def y1_copy(m):
        return remote(y1tx.at[m], y1rx.at[m], y1_s.at[m], y1_r.at[m], 2 * p1 + core, c)

    def y2_copy(m):
        return remote(y2tx.at[m], y2rx.at[m], y2_s.at[m], y2_r.at[m], 2 * p2 + core, c)

    def z_copy(m, k):
        to = (c + k) % 8
        return remote(zst.at[to, m], zrx.at[c, m], z_s.at[k, m], z_r.at[k, m], r, to)

    def z_arrival(m, k):
        src = (c + 8 - k) % 8
        return remote(zst.at[src, m], zrx.at[src, m], z_s.at[k, m], z_r.at[k, m], r, src)

    def step_y1(m):
        core_copy(m).wait_recv()

        def both(j):
            return stage[m, core, j].astype(F32) + crx[m, j].astype(F32)

        y1tx[m, 0] = both(p1).astype(BF16)
        y1tx[m, 1] = both(far).astype(BF16)
        y1_copy(m).start()
        y1own[m, 0] = both(y)
        y1own[m, 1] = both(p2)

    def step_y2(m):
        y1_copy(m).wait_recv()
        y2tx[m] = (y1own[m, 1] + y1rx[m, 1].astype(F32)).astype(BF16)
        y2_copy(m).start()
        y2own[m] = y1own[m, 0] + y1rx[m, 0].astype(F32)

    def step_z(m):
        y2_copy(m).wait_recv()
        t32[0:CHUNK, :] = y2own[m] + y2rx[m].astype(F32)
        for k in range(8):
            piece = t32[k * OWN : k * OWN + PIECE, :].astype(BF16)
            zst[k, m] = piece
        for k in range(1, 8):
            z_copy(m, k).start()
        zrx[c, m] = zst[c, m]

    for copy in x_halo():
        copy.start()
    for copy in x_halo():
        copy.wait_recv()
    for n in range(N_EX):
        load_x(n).wait()
    clear(xp, xcol, xcor, None)

    def first(n, carry):
        spread(xp, xcol, xcor, n)
        load_cot(n).wait()
        acc[...] = conv(w_ref)
        z = acc[...] + b_ref[...]
        s = 1.0 / (1.0 + jnp.exp(-z))
        slope = s * (1.0 + z * (1.0 - s))
        g = (cot[n].reshape(PIX, CH).astype(F32) * slope).astype(BF16)
        gp[n, 1 : TILE + 1] = g.reshape(TILE, TILE, CH)
        wide_g = g.astype(F32)
        g32[...] = wide_g
        bpart[n] = jnp.sum(wide_g.reshape(PIX // 8, 8, CH), axis=0)
        ge[0, n] = g32[pl.ds(0, TILE, stride=TILE), :].astype(BF16)
        ge[1, n] = g32[pl.ds(TILE - 1, TILE, stride=TILE), :].astype(BF16)
        for k, at in enumerate((0, TILE - 1, PIX - TILE, PIX - 1)):
            gc[k, n] = jnp.broadcast_to(g32[at : at + 1, :], (16, CH)).astype(BF16)
        for copy in g_halo(n):
            copy.start()
        gt[...] = gp[n, 1 : TILE + 1].reshape(PIX, CH).T
        for a in range(3):
            part = jnp.dot(
                gt[...], taps[a : a + TILE].reshape(PIX, 3 * CH), preferred_element_type=F32
            )
            for b in range(3):
                block = part[:, b * CH : (b + 1) * CH].T.astype(BF16)
                for k in range(8):
                    group = (3 * a + b) * 8 + k
                    owner, at = group // 9, group % 9 * 16
                    stage[n, owner % 2, owner // 2, at : at + 16, :] = block[16 * k : 16 * k + 16]
        core_copy(n).start()

        @pl.when(n >= 1)
        def _():
            step_y1(n - 1)

        @pl.when(n >= 3)
        def _():
            step_y2(n - 3)

        @pl.when(n >= 5)
        def _():
            step_z(n - 5)

        return carry

    lax.fori_loop(0, N_EX, first, 0)

    def store_out(n):
        return pltpu.make_async_copy(outb.at[n], out_hbm.at[n], lo_s.at[n])

    plan = {
        0: ((step_z, 3), (step_y2, 5)),
        1: ((step_y1, 7),),
        2: ((step_z, 4), (step_y2, 6)),
        3: ((step_z, 5),),
        5: ((step_z, 6), (step_y2, 7)),
        7: ((step_z, 7),),
    }

    def second(n, carry):
        for copy in g_halo(n):
            copy.wait_recv()
        clear(gp, gcol, gcor, n)
        spread(gp, gcol, gcor, n)
        outb[n] = conv(wback).astype(BF16).reshape(TILE, TILE, CH)
        store_out(n).start()
        for when, steps in plan.items():

            @pl.when(n == when)
            def _(steps=steps):
                for step, m in steps:
                    step(m)

        return carry

    lax.fori_loop(0, N_EX, second, 0)

    keep = lax.broadcasted_iota(jnp.int32, (8, CH), 0) < OWN - 16
    for m in range(N_EX):
        for k in range(1, 8):
            z_arrival(m, k).wait_recv()
        total = zrx[0, m].astype(F32)
        for k in range(1, 8):
            total = total + zrx[k, m].astype(F32)
        zacc[m] = total[0:24]
        square = total * total
        part = square[0:8] + square[8:16] + jnp.where(keep, square[16:24], 0.0)
        n1st[m : m + 1, :] = jnp.sum(part, axis=0, keepdims=True)
        n1st[N_EX + m : N_EX + m + 1, :] = jnp.sum(bpart[m], axis=0, keepdims=True)

    def n1_copy(k):
        return remote(n1st, n1rx.at[c], n1_s.at[k], n1_r.at[k], r, (c + k) % 8)

    def n1_arrival(k):
        return remote(n1st, n1rx.at[(c + 8 - k) % 8], n1_s.at[k], n1_r.at[k], r, (c + 8 - k) % 8)

    def n2_copy(k):
        return remote(n2st, n2rx.at[r], n2_s.at[k], n2_r.at[k], (r + k) % 8, c)

    def n2_arrival(k):
        return remote(n2st, n2rx.at[(r + 8 - k) % 8], n2_s.at[k], n2_r.at[k], (r + 8 - k) % 8, c)

    def e_copy(k):
        return remote(est, erx.at[e], e_s.at[k], e_r.at[k], r, c, (e + k) % 4)

    def e_arrival(k):
        return remote(est, erx.at[(e + 4 - k) % 4], e_s.at[k], e_r.at[k], r, c, (e + 4 - k) % 4)

    for k in (4, 3, 5, 2, 6, 1, 7):
        n1_copy(k).start()
    n1rx[c] = n1st[...]
    for k in range(1, 8):
        n1_arrival(k).wait_recv()
    total = n1rx[0]
    for k in range(1, 8):
        total = total + n1rx[k]
    n2st[...] = total
    for k in (4, 3, 5, 2, 6, 1, 7):
        n2_copy(k).start()
    n2rx[r] = total
    for k in range(1, 8):
        n2_arrival(k).wait_recv()
    total = n2rx[0]
    for k in range(1, 8):
        total = total + n2rx[k]
    bias_sum = total[N_EX:]
    squares = jnp.sum(total[0:N_EX] + bias_sum * bias_sum, axis=1, keepdims=True)
    factor = jnp.minimum(1.0, clip / jnp.sqrt(squares + epsilon))
    fst[...] = jnp.broadcast_to(factor, (N_EX, CH))
    weighted = fst[0:1, :] * zacc[0]
    for m in range(1, N_EX):
        weighted = weighted + fst[m : m + 1, :] * zacc[m]
    est[...] = weighted
    est[OWN : OWN + 1, :] = jnp.sum(fst[...] * bias_sum, axis=0, keepdims=True)
    for k in (2, 1, 3):
        e_copy(k).start()
    erx[e] = est[...]
    for k in range(1, 4):
        e_arrival(k).wait_recv()
    total = (erx[0] + erx[1]) + (erx[2] + erx[3])
    gw_ref[...] = (total[0:OWN] + noise_multiplier * clip * nw_ref[...]) * scale
    gb_ref[...] = (total[OWN : OWN + 1] + noise_multiplier * clip * nb_ref[...]) * scale

    for copy in x_halo():
        copy.wait_send()

    def drain(n, carry):
        for copy in g_halo(n):
            copy.wait_send()
        core_copy(n).wait_send()
        y1_copy(n).wait_send()
        y2_copy(n).wait_send()
        for k in range(1, 8):
            z_copy(n, k).wait_send()
        store_out(n).wait()
        return carry

    lax.fori_loop(0, N_EX, drain, 0)
    for k in range(1, 8):
        n1_copy(k).wait_send()
        n2_copy(k).wait_send()
    for k in range(1, 4):
        e_copy(k).wait_send()


def local(inputs, cotangent, weight, bias, noise_weight, noise_bias):
    examples, tile_rows, tile_cols, channels = inputs.shape
    height = tile_rows * lax.axis_size("row")
    width = tile_cols * lax.axis_size("col")
    clip = math.sqrt(height * width * 9 * channels * channels)
    scale = 1.0 / math.sqrt(examples * lax.axis_size("ex") * height * width)
    edges = jnp.stack([inputs[:, :, 0], inputs[:, :, -1]])
    spots = jnp.stack([inputs[:, i, j] for i in (0, -1) for j in (0, -1)])
    spots = jnp.broadcast_to(spots[:, :, None], (4, examples, 16, channels))
    vmem, anywhere = pl.BlockSpec(memory_space=pltpu.VMEM), pl.BlockSpec(memory_space=pl.ANY)
    halo_col, halo_cor = pltpu.VMEM((2, N_EX, TILE, CH), BF16), pltpu.VMEM((4, N_EX, 16, CH), BF16)
    dma = pltpu.SemaphoreType.DMA
    input_grad, grad_weight, grad_bias = pl.pallas_call(
        functools.partial(kernel, clip, scale),
        out_shape=(
            jax.ShapeDtypeStruct(inputs.shape, BF16),
            jax.ShapeDtypeStruct(noise_weight.shape, F32),
            jax.ShapeDtypeStruct((1, channels), F32),
        ),
        in_specs=[anywhere, anywhere] + [vmem] * 6,
        out_specs=[anywhere, vmem, vmem],
        scratch_shapes=[
            pltpu.VMEM((N_EX, TILE + 2, TILE, CH), BF16),
            pltpu.VMEM((N_EX, TILE, TILE, CH), BF16),
            pltpu.VMEM((N_EX, TILE + 2, TILE, CH), BF16),
            halo_col, halo_cor, halo_col, halo_cor, halo_col, halo_cor,
            pltpu.VMEM(((TILE + 2) * PITCH, CH), F32),
            pltpu.VMEM((TILE + 2, TILE, 3 * CH), BF16),
            pltpu.VMEM((CH, PIX), BF16),
            pltpu.VMEM((PIX, CH), F32),
            pltpu.VMEM((3, 3 * CH, CH), BF16),
            pltpu.VMEM((PIX, CH), F32),
            pltpu.VMEM((N_EX, TILE, TILE, CH), BF16),
            pltpu.VMEM((N_EX, 2, 4, CHUNK, CH), BF16),
            pltpu.VMEM((N_EX, 4, CHUNK, CH), BF16),
            pltpu.VMEM((N_EX, 2, CHUNK, CH), F32),
            pltpu.VMEM((N_EX, 2, CHUNK, CH), BF16),
            pltpu.VMEM((N_EX, 2, CHUNK, CH), BF16),
            pltpu.VMEM((N_EX, CHUNK, CH), F32),
            pltpu.VMEM((N_EX, CHUNK, CH), BF16),
            pltpu.VMEM((N_EX, CHUNK, CH), BF16),
            pltpu.VMEM((CHUNK + 16, CH), F32),
            pltpu.VMEM((8, N_EX, PIECE, CH), BF16),
            pltpu.VMEM((8, N_EX, PIECE, CH), BF16),
            pltpu.VMEM((N_EX, 24, CH), F32),
            pltpu.VMEM((N_EX, 8, CH), F32),
            pltpu.VMEM((2 * N_EX, CH), F32),
            pltpu.VMEM((8, 2 * N_EX, CH), F32),
            pltpu.VMEM((2 * N_EX, CH), F32),
            pltpu.VMEM((8, 2 * N_EX, CH), F32),
            pltpu.VMEM((N_EX, CH), F32),
            pltpu.VMEM((24, CH), F32),
            pltpu.VMEM((4, 24, CH), F32),
            dma((N_EX,)), dma((N_EX,)), dma((N_EX,)),
            dma((8,)), dma((8,)), dma((8, N_EX)), dma((8, N_EX)),
            dma((N_EX,)), dma((N_EX,)), dma((N_EX,)), dma((N_EX,)), dma((N_EX,)), dma((N_EX,)),
            dma((8, N_EX)), dma((8, N_EX)),
            dma((8,)), dma((8,)), dma((8,)), dma((8,)), dma((4,)), dma((4,)),
        ],
        compiler_params=pltpu.CompilerParams(
            collective_id=0, has_side_effects=True, vmem_limit_bytes=48 * 2**20
        ),
        name="clipped_grad",
    )(
        inputs, cotangent, weight.reshape(3, 3 * channels, channels), bias.reshape(1, channels),
        noise_weight, noise_bias.reshape(1, channels), edges, spots,
    )
    return input_grad, grad_weight, grad_bias.reshape(channels)


def solution(mesh):
    in_specs = (
        P("ex", "row", "col", None),
        P("ex", "row", "col", None),
        P(),
        P(),
        P(("row", "col"), None),
        P(),
    )
    out_specs = (P("ex", "row", "col", None), P(("row", "col"), None), P())
    return jax.shard_map(local, mesh=mesh, in_specs=in_specs, out_specs=out_specs, check_vma=False)
```

```python
import functools
import math

import jax
import jax.numpy as jnp
from jax import lax
from jax.experimental import pallas as pl
from jax.experimental.pallas import tpu as pltpu
from jax.sharding import PartitionSpec as P

noise_multiplier = 0.002
epsilon = 1e-06
F32 = jnp.float32
BF16 = jnp.bfloat16
N_EX = 8
TILE = 32
CH = 128
PITCH = 48
PIX = TILE * TILE
ROWS = 9 * CH
CHUNK = ROWS // 8
OWN = CHUNK // 8
PIECE = 32


def kernel(
    clip,
    x_hbm, cot_hbm, w_hbm, b_hbm,
    out_hbm, sum_ref,
    w_ref, b_ref, xe_ref, xc_ref, edge, xp, cot, gp, xcol, xcor, gcol, gcor, ge, gc, wide, taps, gt, g32, wback, acc, outb,
    stage, crx, y1own, y1tx, y1rx, y2own, y2tx, y2rx, t32, zst, zrx, zacc, bpart,
    n1st, n1rx, n2st, n2rx, fst, est, erx,
    lw_s, lx_s, lc_s, lo_s, xh_s, xh_r, gh_s, gh_r, c_s, c_r, y1_s, y1_r, y2_s, y2_r, z_s, z_r,
    n1_s, n1_r, n2_s, n2_r, e_s, e_r,
):
    e, r, c = lax.axis_index("ex"), lax.axis_index("row"), lax.axis_index("col")
    core, y = r % 2, r // 2
    up, down, left, right = (r + 7) % 8, (r + 1) % 8, (c + 7) % 8, (c + 1) % 8
    mate = r + 1 - 2 * core
    flip, mirror = y + 1 - 2 * (y % 2), 3 - y
    p1 = flip + core * (mirror - flip)
    p2 = mirror + core * (flip - mirror)
    far = (y + 2) % 4
    corners = ((up, left), (up, right), (down, left), (down, right))

    def remote(src, dst, s_sem, r_sem, to_row, to_col, to_ex=None):
        return pltpu.make_async_remote_copy(
            src_ref=src, dst_ref=dst, send_sem=s_sem, recv_sem=r_sem,
            device_id=(e if to_ex is None else to_ex, to_row, to_col),
            device_id_type=pl.DeviceIdType.MESH,
        )

    def load_x(n):
        return pltpu.make_async_copy(x_hbm.at[n], xp.at[n, 1 : TILE + 1], lx_s.at[n])

    def load_cot(n):
        return pltpu.make_async_copy(cot_hbm.at[n], cot.at[n], lc_s.at[n])

    load_w = pltpu.make_async_copy(w_hbm, w_ref, lw_s.at[0])
    load_b = pltpu.make_async_copy(b_hbm, b_ref, lw_s.at[1])
    for n in range(N_EX):
        load_x(n).start()
    load_w.start()
    load_b.start()
    for n in range(N_EX):
        load_cot(n).start()

    barrier = pltpu.get_barrier_semaphore()
    partners = list(corners)
    partners += [((r + k) % 8, c) for k in range(1, 8)]
    partners += [(r, (c + k) % 8) for k in range(1, 8)]
    for to_row, to_col in partners:
        pl.semaphore_signal(barrier, inc=1, device_id=(e, to_row, to_col), device_id_type=pl.DeviceIdType.MESH)
    for k in range(1, 4):
        pl.semaphore_signal(barrier, inc=1, device_id=((e + k) % 4, r, c), device_id_type=pl.DeviceIdType.MESH)

    def take_edges(n, carry):
        load_x(n).wait()
        for side in range(2):
            block = xp[n, 1 : TILE + 1, side * 16 : side * 16 + 16, :].astype(F32)
            edge[...] = block.reshape(TILE * 16, CH)
            column = edge[pl.ds(15 * side, TILE, stride=16), :]
            xe_ref[side, n] = column.astype(BF16)
            xc_ref[side, n] = jnp.broadcast_to(column[0:1], (16, CH)).astype(BF16)
            xc_ref[2 + side, n] = jnp.broadcast_to(column[TILE - 1 : TILE], (16, CH)).astype(BF16)
        return carry

    lax.fori_loop(0, N_EX, take_edges, 0)
    load_w.wait()
    load_b.wait()
    for a in range(3):
        for b in range(3):
            wback[2 - a, (2 - b) * CH : (3 - b) * CH, :] = w_ref[a, b * CH : (b + 1) * CH, :].T
    t32[...] = jnp.zeros_like(t32)
    pl.semaphore_wait(barrier, 21)

    def x_halo():
        copies = [
            remote(x_hbm.at[:, TILE - 1], xp.at[:, 0], xh_s.at[0], xh_r.at[0], down, c),
            remote(x_hbm.at[:, 0], xp.at[:, TILE + 1], xh_s.at[1], xh_r.at[1], up, c),
            remote(xe_ref.at[1], xcol.at[0], xh_s.at[2], xh_r.at[2], r, right),
            remote(xe_ref.at[0], xcol.at[1], xh_s.at[3], xh_r.at[3], r, left),
        ]
        for k, (to_row, to_col) in enumerate(corners):
            copies.append(
                remote(xc_ref.at[k], xcor.at[3 - k], xh_s.at[4 + k], xh_r.at[7 - k], to_row, to_col)
            )
        return copies

    def g_halo(n):
        copies = [
            remote(gp.at[n, TILE], gp.at[n, 0], gh_s.at[0, n], gh_r.at[0, n], down, c),
            remote(gp.at[n, 1], gp.at[n, TILE + 1], gh_s.at[1, n], gh_r.at[1, n], up, c),
            remote(ge.at[1, n], gcol.at[0, n], gh_s.at[2, n], gh_r.at[2, n], r, right),
            remote(ge.at[0, n], gcol.at[1, n], gh_s.at[3, n], gh_r.at[3, n], r, left),
        ]
        for k, (to_row, to_col) in enumerate(corners):
            copies.append(
                remote(gc.at[k, n], gcor.at[3 - k, n], gh_s.at[4 + k, n], gh_r.at[7 - k, n], to_row, to_col)
            )
        return copies

    def clear(pad, col, cor, n):
        count, at = (N_EX, slice(None)) if n is None else (1, pl.ds(n, 1))
        row_zero = jnp.zeros((count, 1, TILE, CH), BF16)
        col_zero = jnp.zeros((1, count, TILE, CH), BF16)
        cor_zero = jnp.zeros((1, count, 16, CH), BF16)

        @pl.when(r == 0)
        def _():
            pad[at, 0:1] = row_zero
            cor[0:1, at] = cor_zero
            cor[1:2, at] = cor_zero

        @pl.when(r == 7)
        def _():
            pad[at, TILE + 1 : TILE + 2] = row_zero
            cor[2:3, at] = cor_zero
            cor[3:4, at] = cor_zero

        @pl.when(c == 0)
        def _():
            col[0:1, at] = col_zero
            cor[0:1, at] = cor_zero
            cor[2:3, at] = cor_zero

        @pl.when(c == 7)
        def _():
            col[1:2, at] = col_zero
            cor[1:2, at] = cor_zero
            cor[3:4, at] = cor_zero

    def spread(pad, col, cor, n):
        tile = wide.reshape(TILE + 2, PITCH, CH)
        tile[:, 8 : 8 + TILE, :] = pad[n].astype(F32)
        for side, slot in ((0, 7), (1, 8 + TILE)):
            wide[pl.ds(PITCH + slot, TILE, stride=PITCH), :] = col[side, n].astype(F32)
            wide[slot : slot + 1, :] = cor[side, n].astype(F32)[0:1]
            last = (TILE + 1) * PITCH + slot
            wide[last : last + 1, :] = cor[2 + side, n].astype(F32)[0:1]
        taps[:, :, CH : 2 * CH] = pad[n]
        taps[:, :, 0:CH] = tile[:, 7 : 7 + TILE, :].astype(BF16)
        taps[:, :, 2 * CH :] = tile[:, 9 : 9 + TILE, :].astype(BF16)

    def conv(weights):
        total = None
        for a in range(3):
            part = jnp.dot(
                taps[a : a + TILE].reshape(PIX, 3 * CH), weights[a], preferred_element_type=F32
            )
            total = part if total is None else total + part
        return total

    def core_copy(m):
        return remote(stage.at[m, 1 - core], crx.at[m], c_s.at[m], c_r.at[m], mate, c)

    def y1_copy(m):
        return remote(y1tx.at[m], y1rx.at[m], y1_s.at[m], y1_r.at[m], 2 * p1 + core, c)

    def y2_copy(m):
        return remote(y2tx.at[m], y2rx.at[m], y2_s.at[m], y2_r.at[m], 2 * p2 + core, c)

    def z_copy(m, k):
        to = (c + k) % 8
        return remote(zst.at[to, m], zrx.at[c, m], z_s.at[k, m], z_r.at[k, m], r, to)

    def z_arrival(m, k):
        src = (c + 8 - k) % 8
        return remote(zst.at[src, m], zrx.at[src, m], z_s.at[k, m], z_r.at[k, m], r, src)

    def step_y1(m):
        core_copy(m).wait_recv()

        def both(j):
            return stage[m, core, j].astype(F32) + crx[m, j].astype(F32)

        y1tx[m, 0] = both(p1).astype(BF16)
        y1tx[m, 1] = both(far).astype(BF16)
        y1_copy(m).start()
        y1own[m, 0] = both(y)
        y1own[m, 1] = both(p2)

    def step_y2(m):
        y1_copy(m).wait_recv()
        y2tx[m] = (y1own[m, 1] + y1rx[m, 1].astype(F32)).astype(BF16)
        y2_copy(m).start()
        y2own[m] = y1own[m, 0] + y1rx[m, 0].astype(F32)

    def step_z(m):
        y2_copy(m).wait_recv()
        t32[0:CHUNK, :] = y2own[m] + y2rx[m].astype(F32)
        for k in range(8):
            piece = t32[k * OWN : k * OWN + PIECE, :].astype(BF16)
            zst[k, m] = piece
        for k in range(1, 8):
            z_copy(m, k).start()
        zrx[c, m] = zst[c, m]

    for copy in x_halo():
        copy.start()
    for copy in x_halo():
        copy.wait_recv()
    clear(xp, xcol, xcor, None)

    def first(n, carry):
        spread(xp, xcol, xcor, n)
        load_cot(n).wait()
        acc[...] = conv(w_ref)
        z = acc[...] + b_ref[...]
        s = 1.0 / (1.0 + jnp.exp(-z))
        slope = s * (1.0 + z * (1.0 - s))
        g = (cot[n].reshape(PIX, CH).astype(F32) * slope).astype(BF16)
        gp[n, 1 : TILE + 1] = g.reshape(TILE, TILE, CH)
        wide_g = g.astype(F32)
        g32[...] = wide_g
        bpart[n] = jnp.sum(wide_g.reshape(PIX // 8, 8, CH), axis=0)
        ge[0, n] = g32[pl.ds(0, TILE, stride=TILE), :].astype(BF16)
        ge[1, n] = g32[pl.ds(TILE - 1, TILE, stride=TILE), :].astype(BF16)
        for k, at in enumerate((0, TILE - 1, PIX - TILE, PIX - 1)):
            gc[k, n] = jnp.broadcast_to(g32[at : at + 1, :], (16, CH)).astype(BF16)
        for copy in g_halo(n):
            copy.start()
        gt[...] = gp[n, 1 : TILE + 1].reshape(PIX, CH).T
        for a in range(3):
            part = jnp.dot(
                gt[...], taps[a : a + TILE].reshape(PIX, 3 * CH), preferred_element_type=F32
            )
            for b in range(3):
                block = part[:, b * CH : (b + 1) * CH].T.astype(BF16)
                for k in range(8):
                    group = (3 * a + b) * 8 + k
                    owner, at = group // 9, group % 9 * 16
                    stage[n, owner % 2, owner // 2, at : at + 16, :] = block[16 * k : 16 * k + 16]
        core_copy(n).start()

        @pl.when(n >= 1)
        def _():
            step_y1(n - 1)

        @pl.when(n >= 3)
        def _():
            step_y2(n - 3)

        @pl.when(n >= 5)
        def _():
            step_z(n - 5)

        return carry

    lax.fori_loop(0, N_EX, first, 0)

    def store_out(n):
        return pltpu.make_async_copy(outb.at[n], out_hbm.at[n], lo_s.at[n])

    plan = {
        0: ((step_z, 3), (step_y2, 5)),
        1: ((step_y1, 7),),
        2: ((step_z, 4), (step_y2, 6)),
        3: ((step_z, 5),),
        5: ((step_z, 6), (step_y2, 7)),
        7: ((step_z, 7),),
    }

    def second(n, carry):
        for copy in g_halo(n):
            copy.wait_recv()
        clear(gp, gcol, gcor, n)
        spread(gp, gcol, gcor, n)
        outb[n] = conv(wback).astype(BF16).reshape(TILE, TILE, CH)
        store_out(n).start()
        for when, steps in plan.items():

            @pl.when(n == when)
            def _(steps=steps):
                for step, m in steps:
                    step(m)

        return carry

    lax.fori_loop(0, N_EX, second, 0)

    keep = lax.broadcasted_iota(jnp.int32, (8, CH), 0) < OWN - 16
    for m in range(N_EX):
        for k in range(1, 8):
            z_arrival(m, k).wait_recv()
        total = zrx[0, m].astype(F32)
        for k in range(1, 8):
            total = total + zrx[k, m].astype(F32)
        zacc[m] = total[0:24]
        square = total * total
        part = square[0:8] + square[8:16] + jnp.where(keep, square[16:24], 0.0)
        n1st[m : m + 1, :] = jnp.sum(part, axis=0, keepdims=True)
        n1st[N_EX + m : N_EX + m + 1, :] = jnp.sum(bpart[m], axis=0, keepdims=True)

    def n1_copy(k):
        return remote(n1st, n1rx.at[c], n1_s.at[k], n1_r.at[k], r, (c + k) % 8)

    def n1_arrival(k):
        return remote(n1st, n1rx.at[(c + 8 - k) % 8], n1_s.at[k], n1_r.at[k], r, (c + 8 - k) % 8)

    def n2_copy(k):
        return remote(n2st, n2rx.at[r], n2_s.at[k], n2_r.at[k], (r + k) % 8, c)

    def n2_arrival(k):
        return remote(n2st, n2rx.at[(r + 8 - k) % 8], n2_s.at[k], n2_r.at[k], (r + 8 - k) % 8, c)

    def e_copy(k):
        return remote(est, erx.at[e], e_s.at[k], e_r.at[k], r, c, (e + k) % 4)

    def e_arrival(k):
        return remote(est, erx.at[(e + 4 - k) % 4], e_s.at[k], e_r.at[k], r, c, (e + 4 - k) % 4)

    for k in (4, 3, 5, 2, 6, 1, 7):
        n1_copy(k).start()
    n1rx[c] = n1st[...]
    for k in range(1, 8):
        n1_arrival(k).wait_recv()
    total = n1rx[0]
    for k in range(1, 8):
        total = total + n1rx[k]
    n2st[...] = total
    for k in (4, 3, 5, 2, 6, 1, 7):
        n2_copy(k).start()
    n2rx[r] = total
    for k in range(1, 8):
        n2_arrival(k).wait_recv()
    total = n2rx[0]
    for k in range(1, 8):
        total = total + n2rx[k]
    bias_sum = total[N_EX:]
    squares = jnp.sum(total[0:N_EX] + bias_sum * bias_sum, axis=1, keepdims=True)
    factor = jnp.minimum(1.0, clip / jnp.sqrt(squares + epsilon))
    fst[...] = jnp.broadcast_to(factor, (N_EX, CH))
    weighted = fst[0:1, :] * zacc[0]
    for m in range(1, N_EX):
        weighted = weighted + fst[m : m + 1, :] * zacc[m]
    est[...] = weighted
    est[OWN : OWN + 1, :] = jnp.sum(fst[...] * bias_sum, axis=0, keepdims=True)
    for k in (2, 1, 3):
        e_copy(k).start()
    erx[e] = est[...]
    for k in range(1, 4):
        e_arrival(k).wait_recv()
    sum_ref[...] = (erx[0] + erx[1]) + (erx[2] + erx[3])

    for copy in x_halo():
        copy.wait_send()

    def drain(n, carry):
        for copy in g_halo(n):
            copy.wait_send()
        core_copy(n).wait_send()
        y1_copy(n).wait_send()
        y2_copy(n).wait_send()
        for k in range(1, 8):
            z_copy(n, k).wait_send()
        store_out(n).wait()
        return carry

    lax.fori_loop(0, N_EX, drain, 0)
    for k in range(1, 8):
        n1_copy(k).wait_send()
        n2_copy(k).wait_send()
    for k in range(1, 4):
        e_copy(k).wait_send()


def local(inputs, cotangent, weight, bias, noise_weight, noise_bias):
    examples, tile_rows, tile_cols, channels = inputs.shape
    height = tile_rows * lax.axis_size("row")
    width = tile_cols * lax.axis_size("col")
    clip = math.sqrt(height * width * 9 * channels * channels)
    scale = 1.0 / math.sqrt(examples * lax.axis_size("ex") * height * width)
    vmem, anywhere = pl.BlockSpec(memory_space=pltpu.VMEM), pl.BlockSpec(memory_space=pl.ANY)
    halo_col, halo_cor = pltpu.VMEM((2, N_EX, TILE, CH), BF16), pltpu.VMEM((4, N_EX, 16, CH), BF16)
    dma = pltpu.SemaphoreType.DMA
    input_grad, total = pl.pallas_call(
        functools.partial(kernel, clip),
        out_shape=(
            jax.ShapeDtypeStruct(inputs.shape, BF16),
            jax.ShapeDtypeStruct((24, channels), F32),
        ),
        in_specs=[pl.BlockSpec(memory_space=pltpu.MemorySpace.HBM)] * 4,
        out_specs=[anywhere, vmem],
        scratch_shapes=[
            pltpu.VMEM((3, 3 * CH, CH), BF16),
            pltpu.VMEM((1, CH), F32),
            halo_col, halo_cor,
            pltpu.VMEM((TILE * 16, CH), F32),
            pltpu.VMEM((N_EX, TILE + 2, TILE, CH), BF16),
            pltpu.VMEM((N_EX, TILE, TILE, CH), BF16),
            pltpu.VMEM((N_EX, TILE + 2, TILE, CH), BF16),
            halo_col, halo_cor, halo_col, halo_cor, halo_col, halo_cor,
            pltpu.VMEM(((TILE + 2) * PITCH, CH), F32),
            pltpu.VMEM((TILE + 2, TILE, 3 * CH), BF16),
            pltpu.VMEM((CH, PIX), BF16),
            pltpu.VMEM((PIX, CH), F32),
            pltpu.VMEM((3, 3 * CH, CH), BF16),
            pltpu.VMEM((PIX, CH), F32),
            pltpu.VMEM((N_EX, TILE, TILE, CH), BF16),
            pltpu.VMEM((N_EX, 2, 4, CHUNK, CH), BF16),
            pltpu.VMEM((N_EX, 4, CHUNK, CH), BF16),
            pltpu.VMEM((N_EX, 2, CHUNK, CH), F32),
            pltpu.VMEM((N_EX, 2, CHUNK, CH), BF16),
            pltpu.VMEM((N_EX, 2, CHUNK, CH), BF16),
            pltpu.VMEM((N_EX, CHUNK, CH), F32),
            pltpu.VMEM((N_EX, CHUNK, CH), BF16),
            pltpu.VMEM((N_EX, CHUNK, CH), BF16),
            pltpu.VMEM((CHUNK + 16, CH), F32),
            pltpu.VMEM((8, N_EX, PIECE, CH), BF16),
            pltpu.VMEM((8, N_EX, PIECE, CH), BF16),
            pltpu.VMEM((N_EX, 24, CH), F32),
            pltpu.VMEM((N_EX, 8, CH), F32),
            pltpu.VMEM((2 * N_EX, CH), F32),
            pltpu.VMEM((8, 2 * N_EX, CH), F32),
            pltpu.VMEM((2 * N_EX, CH), F32),
            pltpu.VMEM((8, 2 * N_EX, CH), F32),
            pltpu.VMEM((N_EX, CH), F32),
            pltpu.VMEM((24, CH), F32),
            pltpu.VMEM((4, 24, CH), F32),
            dma((2,)), dma((N_EX,)), dma((N_EX,)), dma((N_EX,)),
            dma((8,)), dma((8,)), dma((8, N_EX)), dma((8, N_EX)),
            dma((N_EX,)), dma((N_EX,)), dma((N_EX,)), dma((N_EX,)), dma((N_EX,)), dma((N_EX,)),
            dma((8, N_EX)), dma((8, N_EX)),
            dma((8,)), dma((8,)), dma((8,)), dma((8,)), dma((4,)), dma((4,)),
        ],
        compiler_params=pltpu.CompilerParams(
            collective_id=0, has_side_effects=True
        ),
        name="clipped_grad",
    )(
        inputs, cotangent, weight.reshape(3, 3 * channels, channels), bias.reshape(1, channels)
    )
    grad_weight = (total[0:OWN] + noise_multiplier * clip * noise_weight) * scale
    grad_bias = (total[OWN] + noise_multiplier * clip * noise_bias) * scale
    return input_grad, grad_weight, grad_bias


def solution(mesh):
    in_specs = (
        P("ex", "row", "col", None),
        P("ex", "row", "col", None),
        P(),
        P(),
        P(("row", "col"), None),
        P(),
    )
    out_specs = (P("ex", "row", "col", None), P(("row", "col"), None), P())
    return jax.shard_map(local, mesh=mesh, in_specs=in_specs, out_specs=out_specs, check_vma=False)
```

```python
import functools
import math

import jax
import jax.numpy as jnp
from jax import lax
from jax.experimental import pallas as pl
from jax.experimental.pallas import tpu as pltpu
from jax.sharding import PartitionSpec as P

noise_multiplier = 0.002
epsilon = 1e-06
F32 = jnp.float32
BF16 = jnp.bfloat16
N_EX = 8
TILE = 32
CH = 128
PITCH = 48
PIX = TILE * TILE
ROWS = 9 * CH
CHUNK = ROWS // 8
OWN = CHUNK // 8
PIECE = 32


def kernel(
    clip,
    x_hbm, cot_hbm, w_hbm, b_hbm,
    out_hbm, sum_ref,
    w_ref, b_ref, xe_ref, xc_ref, edge, xp, cot, gp, xcol, xcor, gcol, gcor, ge, gc, wide, taps, gt, g32, wback, acc, outb,
    stage, crx, y1own, y1tx, y1rx, y2own, y2tx, y2rx, t32, zst, zrx, zacc, bpart,
    b1st, b1rx, b2st, b2rx, n1st, n1rx, n2st, n2rx, fst, est, erx,
    lw_s, lx_s, lc_s, lo_s, xh_s, xh_r, gh_s, gh_r, c_s, c_r, y1_s, y1_r, y2_s, y2_r, z_s, z_r,
    b1_s, b1_r, b2_s, b2_r, n1_s, n1_r, n2_s, n2_r, e_s, e_r,
):
    e, r, c = lax.axis_index("ex"), lax.axis_index("row"), lax.axis_index("col")
    core, y = r % 2, r // 2
    up, down, left, right = (r + 7) % 8, (r + 1) % 8, (c + 7) % 8, (c + 1) % 8
    mate = r + 1 - 2 * core
    flip, mirror = y + 1 - 2 * (y % 2), 3 - y
    p1 = flip + core * (mirror - flip)
    p2 = mirror + core * (flip - mirror)
    far = (y + 2) % 4
    corners = ((up, left), (up, right), (down, left), (down, right))

    def remote(src, dst, s_sem, r_sem, to_row, to_col, to_ex=None):
        return pltpu.make_async_remote_copy(
            src_ref=src, dst_ref=dst, send_sem=s_sem, recv_sem=r_sem,
            device_id=(e if to_ex is None else to_ex, to_row, to_col),
            device_id_type=pl.DeviceIdType.MESH,
        )

    def received(view, sem):
        remote(view, view, sem, sem, r, c).wait_recv()

    def sent(view, sem):
        remote(view, view, sem, sem, r, c).wait_send()

    def load_x(n):
        return pltpu.make_async_copy(x_hbm.at[n], xp.at[n, 1 : TILE + 1], lx_s.at[n])

    load_w = pltpu.make_async_copy(w_hbm, w_ref, lw_s.at[0])
    load_b = pltpu.make_async_copy(b_hbm, b_ref, lw_s.at[1])
    for n in range(N_EX):
        load_x(n).start()
    load_w.start()
    load_b.start()
    load_cot = pltpu.make_async_copy(cot_hbm, cot, lc_s)
    load_cot.start()

    barrier = pltpu.get_barrier_semaphore()
    partners = list(corners)
    partners += [((r + k) % 8, c) for k in range(1, 8)]
    partners += [(r, (c + k) % 8) for k in range(1, 8)]
    for to_row, to_col in partners:
        pl.semaphore_signal(barrier, inc=1, device_id=(e, to_row, to_col), device_id_type=pl.DeviceIdType.MESH)
    for k in range(1, 4):
        pl.semaphore_signal(barrier, inc=1, device_id=((e + k) % 4, r, c), device_id_type=pl.DeviceIdType.MESH)

    def take_edges(n, carry):
        load_x(n).wait()
        for side in range(2):
            block = xp[n, 1 : TILE + 1, side * 16 : side * 16 + 16, :].astype(F32)
            edge[...] = block.reshape(TILE * 16, CH)
            column = edge[pl.ds(15 * side, TILE, stride=16), :]
            xe_ref[side, n] = column.astype(BF16)
            xc_ref[side, pl.ds(n, 1), :] = column[0:1]
            xc_ref[2 + side, pl.ds(n, 1), :] = column[TILE - 1 : TILE]
        return carry

    lax.fori_loop(0, N_EX, take_edges, 0)
    load_w.wait()
    load_b.wait()
    for a in range(3):
        for b in range(3):
            wback[2 - a, (2 - b) * CH : (3 - b) * CH, :] = w_ref[a, b * CH : (b + 1) * CH, :].T
    t32[...] = jnp.zeros_like(t32)
    pl.semaphore_wait(barrier, 21)

    def x_halo():
        copies = [
            remote(x_hbm.at[:, TILE - 1], xp.at[:, 0], xh_s, xh_r, down, c),
            remote(x_hbm.at[:, 0], xp.at[:, TILE + 1], xh_s, xh_r, up, c),
            remote(xe_ref.at[1], xcol.at[0], xh_s, xh_r, r, right),
            remote(xe_ref.at[0], xcol.at[1], xh_s, xh_r, r, left),
        ]
        for k, (to_row, to_col) in enumerate(corners):
            copies.append(remote(xc_ref.at[k], xcor.at[3 - k], xh_s, xh_r, to_row, to_col))
        return copies

    x_bytes = acc.at[0 : 4 * N_EX * TILE // 2 + 4 * N_EX]

    def g_halo(n):
        copies = [
            remote(gp.at[n, TILE], gp.at[n, 0], gh_s, gh_r.at[n], down, c),
            remote(gp.at[n, 1], gp.at[n, TILE + 1], gh_s, gh_r.at[n], up, c),
            remote(ge.at[1, n], gcol.at[0, n], gh_s, gh_r.at[n], r, right),
            remote(ge.at[0, n], gcol.at[1, n], gh_s, gh_r.at[n], r, left),
        ]
        for k, (to_row, to_col) in enumerate(corners):
            copies.append(remote(gc.at[k, n], gcor.at[3 - k, n], gh_s, gh_r.at[n], to_row, to_col))
        return copies

    def clear(pad, col, cor, n):
        count, at = (N_EX, slice(None)) if n is None else (1, pl.ds(n, 1))
        row_zero = jnp.zeros((count, 1, TILE, CH), BF16)
        col_zero = jnp.zeros((1, count, TILE, CH), BF16)
        cor_zero = jnp.zeros((1, N_EX, CH), F32) if n is None else jnp.zeros((1, 1, 16, CH), BF16)

        @pl.when(r == 0)
        def _():
            pad[at, 0:1] = row_zero
            cor[0:1, at] = cor_zero
            cor[1:2, at] = cor_zero

        @pl.when(r == 7)
        def _():
            pad[at, TILE + 1 : TILE + 2] = row_zero
            cor[2:3, at] = cor_zero
            cor[3:4, at] = cor_zero

        @pl.when(c == 0)
        def _():
            col[0:1, at] = col_zero
            cor[0:1, at] = cor_zero
            cor[2:3, at] = cor_zero

        @pl.when(c == 7)
        def _():
            col[1:2, at] = col_zero
            cor[1:2, at] = cor_zero
            cor[3:4, at] = cor_zero

    def spread(pad, col, spot, n):
        tile = wide.reshape(TILE + 2, PITCH, CH)
        tile[:, 8 : 8 + TILE, :] = pad[n].astype(F32)
        for side, slot in ((0, 7), (1, 8 + TILE)):
            wide[pl.ds(PITCH + slot, TILE, stride=PITCH), :] = col[side, n].astype(F32)
            wide[slot : slot + 1, :] = spot(side)
            last = (TILE + 1) * PITCH + slot
            wide[last : last + 1, :] = spot(2 + side)
        taps[:, :, CH : 2 * CH] = pad[n]
        taps[:, :, 0:CH] = tile[:, 7 : 7 + TILE, :].astype(BF16)
        taps[:, :, 2 * CH :] = tile[:, 9 : 9 + TILE, :].astype(BF16)

    def conv(weights):
        total = None
        for a in range(3):
            part = jnp.dot(
                taps[a : a + TILE].reshape(PIX, 3 * CH), weights[a], preferred_element_type=F32
            )
            total = part if total is None else total + part
        return total

    def core_copy(m):
        return remote(stage.at[m, 1 - core], crx.at[m], c_s, c_r.at[m], mate, c)

    def y1_copy(m):
        return remote(y1tx.at[m], y1rx.at[m], y1_s, y1_r.at[m], 2 * p1 + core, c)

    def y2_copy(m):
        return remote(y2tx.at[m], y2rx.at[m], y2_s, y2_r.at[m], 2 * p2 + core, c)

    def z_copy(m, k):
        to = (c + k) % 8
        return remote(zst.at[to, m], zrx.at[c, m], z_s, z_r, r, to)

    def step_y1(m):
        core_copy(m).wait_recv()

        def both(j):
            return stage[m, core, j].astype(F32) + crx[m, j].astype(F32)

        y1tx[m, 0] = both(p1).astype(BF16)
        y1tx[m, 1] = both(far).astype(BF16)
        y1_copy(m).start()
        y1own[m, 0] = both(y)
        y1own[m, 1] = both(p2)

    def step_y2(m):
        y1_copy(m).wait_recv()
        y2tx[m] = (y1own[m, 1] + y1rx[m, 1].astype(F32)).astype(BF16)
        y2_copy(m).start()
        y2own[m] = y1own[m, 0] + y1rx[m, 0].astype(F32)

    def step_z(m):
        y2_copy(m).wait_recv()
        t32[0:CHUNK, :] = y2own[m] + y2rx[m].astype(F32)
        for k in range(8):
            piece = t32[k * OWN : k * OWN + PIECE, :].astype(BF16)
            zst[k, m] = piece
        for k in range(1, 8):
            z_copy(m, k).start()
        zrx[c, m] = zst[c, m]

    for copy in x_halo():
        copy.start()
    received(x_bytes, xh_r)
    clear(xp, xcol, xcor, None)
    load_cot.wait()

    def first(n, carry):
        spread(xp, xcol, lambda k: xcor[k, pl.ds(n, 1), :], n)
        acc[...] = conv(w_ref)
        half = 0.5 * (acc[...] + b_ref[...])
        t = jnp.tanh(half)
        slope = (1.0 + t) + half * (1.0 - t * t)
        g = (0.5 * cot[n].reshape(PIX, CH).astype(F32) * slope).astype(BF16)
        gp[n, 1 : TILE + 1] = g.reshape(TILE, TILE, CH)
        wide_g = g.astype(F32)
        g32[...] = wide_g
        bpart[n] = jnp.sum(wide_g.reshape(PIX // 8, 8, CH), axis=0)
        ge[0, n] = g32[pl.ds(0, TILE, stride=TILE), :].astype(BF16)
        ge[1, n] = g32[pl.ds(TILE - 1, TILE, stride=TILE), :].astype(BF16)
        for k, at in enumerate((0, TILE - 1, PIX - TILE, PIX - 1)):
            gc[k, n] = jnp.broadcast_to(g32[at : at + 1, :], (16, CH)).astype(BF16)
        for copy in g_halo(n):
            copy.start()
        gt[...] = gp[n, 1 : TILE + 1].reshape(PIX, CH).T
        for a in range(3):
            part = jnp.dot(
                gt[...], taps[a : a + TILE].reshape(PIX, 3 * CH), preferred_element_type=F32
            )
            for b in range(3):
                block = part[:, b * CH : (b + 1) * CH].T.astype(BF16)
                for k in range(8):
                    group = (3 * a + b) * 8 + k
                    owner, at = group // 9, group % 9 * 16
                    stage[n, owner % 2, owner // 2, at : at + 16, :] = block[16 * k : 16 * k + 16]
        core_copy(n).start()

        @pl.when(n >= 1)
        def _():
            step_y1(n - 1)

        @pl.when(n >= 3)
        def _():
            step_y2(n - 3)

        @pl.when(n >= 5)
        def _():
            step_z(n - 5)

        return carry

    lax.fori_loop(0, N_EX, first, 0)

    def store_out(n):
        return pltpu.make_async_copy(outb.at[n], out_hbm.at[n], lo_s)

    def b1_copy(k):
        return remote(b1st, b1rx.at[c], b1_s, b1_r, r, (c + k) % 8)

    def b2_copy(k):
        return remote(b2st, b2rx.at[r], b2_s, b2_r, (r + k) % 8, c)

    def n1_copy(k):
        return remote(n1st, n1rx.at[c], n1_s, n1_r, r, (c + k) % 8)

    def n2_copy(k):
        return remote(n2st, n2rx.at[r], n2_s, n2_r, (r + k) % 8, c)

    def e_copy(k):
        return remote(est, erx.at[e], e_s, e_r, r, c, (e + k) % 4)

    away = (4, 3, 5, 2, 6, 1, 7)

    def add_up(rx):
        total = rx[0]
        for k in range(1, 8):
            total = total + rx[k]
        return total

    def bias_z(_):
        for m in range(N_EX):
            b1st[m : m + 1, :] = jnp.sum(bpart[m], axis=0, keepdims=True)
        b1rx[c] = b1st[...]
        for k in away:
            b1_copy(k).start()

    def bias_row(_):
        received(b1rx.at[0:7], b1_r)
        total = add_up(b1rx)
        b2st[...] = total
        b2rx[r] = total
        for k in away:
            b2_copy(k).start()

    plan = {
        0: ((step_z, 3), (step_y2, 5), (bias_z, 0)),
        1: ((step_y1, 7),),
        2: ((step_z, 4), (step_y2, 6)),
        3: ((step_z, 5),),
        5: ((step_z, 6), (step_y2, 7), (bias_row, 0)),
        7: ((step_z, 7),),
    }

    def second(n, carry):
        received(gp.at[n, 0:6], gh_r.at[n])
        clear(gp, gcol, gcor, n)
        spread(gp, gcol, lambda k: gcor[k, n].astype(F32)[0:1], n)
        outb[n] = conv(wback).astype(BF16).reshape(TILE, TILE, CH)
        store_out(n).start()
        for when, steps in plan.items():

            @pl.when(n == when)
            def _(steps=steps):
                for step, m in steps:
                    step(m)

        return carry

    lax.fori_loop(0, N_EX, second, 0)

    received(b2rx.at[0:7], b2_r)
    bias_sum = add_up(b2rx)
    keep = lax.broadcasted_iota(jnp.int32, (8, CH), 0) < OWN - 16
    own_lane = lax.broadcasted_iota(jnp.int32, (8, CH), 1) // 16 == lax.broadcasted_iota(jnp.int32, (8, CH), 0)
    received(zrx.at[0:7], z_r)
    for m in range(N_EX):
        total = zrx[0, m].astype(F32)
        for k in range(1, 8):
            total = total + zrx[k, m].astype(F32)
        zacc[m] = total[0:24]
        square = total * total
        part = square[0:8] + square[8:16] + jnp.where(keep, square[16:24], 0.0)
        fst[m : m + 1, :] = jnp.sum(part, axis=0, keepdims=True)
    folded = fst[...]
    for width in (64, 32, 16):
        folded = folded + pltpu.roll(folded, width, 1)
    total = jnp.sum(jnp.where(own_lane, folded, 0.0), axis=0, keepdims=True)
    n1st[...] = total
    n1rx[c] = total
    for k in away:
        n1_copy(k).start()
    received(n1rx.at[0:7], n1_r)
    total = add_up(n1rx)
    n2st[...] = total
    n2rx[r] = total
    for k in away:
        n2_copy(k).start()
    received(n2rx.at[0:7], n2_r)
    total = add_up(n2rx)
    squares = jnp.where(own_lane, jnp.broadcast_to(total, (N_EX, CH)), 0.0) + bias_sum * bias_sum
    factor = jnp.minimum(1.0, clip / jnp.sqrt(jnp.sum(squares, axis=1, keepdims=True) + epsilon))
    fst[...] = jnp.broadcast_to(factor, (N_EX, CH))
    weighted = fst[0:1, :] * zacc[0]
    for m in range(1, N_EX):
        weighted = weighted + fst[m : m + 1, :] * zacc[m]
    est[...] = weighted
    est[OWN : OWN + 1, :] = jnp.sum(fst[...] * bias_sum, axis=0, keepdims=True)
    erx[e] = est[...]
    for k in (2, 1, 3):
        e_copy(k).start()
    received(erx.at[0:3], e_r)
    sum_ref[...] = (erx[0] + erx[1]) + (erx[2] + erx[3])

    sent(x_bytes, xh_s)
    sent(gp.at[:, 0:6], gh_s)
    sent(crx, c_s)
    sent(y1tx, y1_s)
    sent(y2tx, y2_s)
    sent(zst.at[0:7], z_s)
    sent(b1rx.at[0:7], b1_s)
    sent(b2rx.at[0:7], b2_s)
    sent(n1rx.at[0:7], n1_s)
    sent(n2rx.at[0:7], n2_s)
    sent(erx.at[0:3], e_s)
    pltpu.make_async_copy(outb, out_hbm, lo_s).wait()


def local(inputs, cotangent, weight, bias, noise_weight, noise_bias):
    examples, tile_rows, tile_cols, channels = inputs.shape
    height = tile_rows * lax.axis_size("row")
    width = tile_cols * lax.axis_size("col")
    clip = math.sqrt(height * width * 9 * channels * channels)
    scale = 1.0 / math.sqrt(examples * lax.axis_size("ex") * height * width)
    vmem, anywhere = pl.BlockSpec(memory_space=pltpu.VMEM), pl.BlockSpec(memory_space=pl.ANY)
    halo_col, halo_cor = pltpu.VMEM((2, N_EX, TILE, CH), BF16), pltpu.VMEM((4, N_EX, 16, CH), BF16)
    spots = pltpu.VMEM((4, N_EX, CH), F32)
    dma = pltpu.SemaphoreType.DMA
    input_grad, total = pl.pallas_call(
        functools.partial(kernel, clip),
        out_shape=(
            jax.ShapeDtypeStruct(inputs.shape, BF16),
            jax.ShapeDtypeStruct((24, channels), F32),
        ),
        in_specs=[pl.BlockSpec(memory_space=pltpu.MemorySpace.HBM)] * 4,
        out_specs=[anywhere, vmem],
        scratch_shapes=[
            pltpu.VMEM((3, 3 * CH, CH), BF16),
            pltpu.VMEM((1, CH), F32),
            halo_col, spots,
            pltpu.VMEM((TILE * 16, CH), F32),
            pltpu.VMEM((N_EX, TILE + 2, TILE, CH), BF16),
            pltpu.VMEM((N_EX, TILE, TILE, CH), BF16),
            pltpu.VMEM((N_EX, TILE + 2, TILE, CH), BF16),
            halo_col, spots, halo_col, halo_cor, halo_col, halo_cor,
            pltpu.VMEM(((TILE + 2) * PITCH, CH), F32),
            pltpu.VMEM((TILE + 2, TILE, 3 * CH), BF16),
            pltpu.VMEM((CH, PIX), BF16),
            pltpu.VMEM((PIX, CH), F32),
            pltpu.VMEM((3, 3 * CH, CH), BF16),
            pltpu.VMEM((PIX, CH), F32),
            pltpu.VMEM((N_EX, TILE, TILE, CH), BF16),
            pltpu.VMEM((N_EX, 2, 4, CHUNK, CH), BF16),
            pltpu.VMEM((N_EX, 4, CHUNK, CH), BF16),
            pltpu.VMEM((N_EX, 2, CHUNK, CH), F32),
            pltpu.VMEM((N_EX, 2, CHUNK, CH), BF16),
            pltpu.VMEM((N_EX, 2, CHUNK, CH), BF16),
            pltpu.VMEM((N_EX, CHUNK, CH), F32),
            pltpu.VMEM((N_EX, CHUNK, CH), BF16),
            pltpu.VMEM((N_EX, CHUNK, CH), BF16),
            pltpu.VMEM((CHUNK + 16, CH), F32),
            pltpu.VMEM((8, N_EX, PIECE, CH), BF16),
            pltpu.VMEM((8, N_EX, PIECE, CH), BF16),
            pltpu.VMEM((N_EX, 24, CH), F32),
            pltpu.VMEM((N_EX, 8, CH), F32),
            pltpu.VMEM((N_EX, CH), F32),
            pltpu.VMEM((8, N_EX, CH), F32),
            pltpu.VMEM((N_EX, CH), F32),
            pltpu.VMEM((8, N_EX, CH), F32),
            pltpu.VMEM((1, CH), F32),
            pltpu.VMEM((8, 1, CH), F32),
            pltpu.VMEM((1, CH), F32),
            pltpu.VMEM((8, 1, CH), F32),
            pltpu.VMEM((N_EX, CH), F32),
            pltpu.VMEM((24, CH), F32),
            pltpu.VMEM((4, 24, CH), F32),
            dma((2,)), dma((N_EX,)), dma(()), dma(()),
            dma(()), dma(()), dma(()), dma((N_EX,)),
            dma(()), dma((N_EX,)), dma(()), dma((N_EX,)), dma(()), dma((N_EX,)), dma(()), dma(()),
            dma(()), dma(()), dma(()), dma(()), dma(()), dma(()), dma(()), dma(()), dma(()), dma(()),
        ],
        compiler_params=pltpu.CompilerParams(
            collective_id=0, has_side_effects=True
        ),
        name="clipped_grad",
    )(
        inputs, cotangent, weight.reshape(3, 3 * channels, channels), bias.reshape(1, channels)
    )
    grad_weight = (total[0:OWN] + noise_multiplier * clip * noise_weight) * scale
    grad_bias = (total[OWN] + noise_multiplier * clip * noise_bias) * scale
    return input_grad, grad_weight, grad_bias


def solution(mesh):
    in_specs = (
        P("ex", "row", "col", None),
        P("ex", "row", "col", None),
        P(),
        P(),
        P(("row", "col"), None),
        P(),
    )
    out_specs = (P("ex", "row", "col", None), P(("row", "col"), None), P())
    return jax.shard_map(local, mesh=mesh, in_specs=in_specs, out_specs=out_specs, check_vma=False)
```

```python
import functools
import math

import jax
import jax.numpy as jnp
from jax import lax
from jax.experimental import pallas as pl
from jax.experimental.pallas import tpu as pltpu
from jax.sharding import PartitionSpec as P

noise_multiplier = 0.002
epsilon = 1e-06
F32 = jnp.float32
BF16 = jnp.bfloat16
N_EX = 8
TILE = 32
CH = 128
PITCH = 48
PIX = TILE * TILE
ROWS = 9 * CH
CHUNK = ROWS // 8
OWN = CHUNK // 8
PIECE = 32


def kernel(
    clip,
    x_hbm, cot_hbm, w_hbm, b_hbm,
    out_ref, sum_ref,
    w_ref, b_ref, xe_ref, xc_ref, edge, xp, cot, gp, xcol, xcor, gcol, gcor, ge, gc, wide, taps, gt, g32, wback, acc,
    stage, crx, y1own, y1tx, y1rx, y2own, y2tx, y2rx, t32, zst, zrx, zacc, bpart,
    b1st, b1rx, b2st, b2rx, n1st, n1rx, n2st, n2rx, fst, est, erx,
    lw_s, lx_s, lc_s, xh_s, xh_r, gh_s, gh_r, c_s, c_r, y1_s, y1_r, y2_s, y2_r, z_s, z_r,
    b1_s, b1_r, b2_s, b2_r, n1_s, n1_r, n2_s, n2_r, e_s, e_r,
):
    e, r, c = lax.axis_index("ex"), lax.axis_index("row"), lax.axis_index("col")
    core, y = r % 2, r // 2
    up, down, left, right = (r + 7) % 8, (r + 1) % 8, (c + 7) % 8, (c + 1) % 8
    mate = r + 1 - 2 * core
    flip, mirror = y + 1 - 2 * (y % 2), 3 - y
    p1 = flip + core * (mirror - flip)
    p2 = mirror + core * (flip - mirror)
    far = (y + 2) % 4
    corners = ((up, left), (up, right), (down, left), (down, right))

    def remote(src, dst, s_sem, r_sem, to_row, to_col, to_ex=None):
        return pltpu.make_async_remote_copy(
            src_ref=src, dst_ref=dst, send_sem=s_sem, recv_sem=r_sem,
            device_id=(e if to_ex is None else to_ex, to_row, to_col),
            device_id_type=pl.DeviceIdType.MESH,
        )

    def received(view, sem):
        remote(view, view, sem, sem, r, c).wait_recv()

    def sent(view, sem):
        remote(view, view, sem, sem, r, c).wait_send()

    def load_x(n):
        return pltpu.make_async_copy(x_hbm.at[n], xp.at[n, 1 : TILE + 1], lx_s.at[n])

    load_w = pltpu.make_async_copy(w_hbm, w_ref, lw_s.at[0])
    load_b = pltpu.make_async_copy(b_hbm, b_ref, lw_s.at[1])
    for n in range(N_EX):
        load_x(n).start()
    load_w.start()
    load_b.start()
    load_cot = pltpu.make_async_copy(cot_hbm, cot, lc_s)
    load_cot.start()

    barrier = pltpu.get_barrier_semaphore()
    partners = list(corners)
    partners += [((r + k) % 8, c) for k in range(1, 8)]
    partners += [(r, (c + k) % 8) for k in range(1, 8)]
    for to_row, to_col in partners:
        pl.semaphore_signal(barrier, inc=1, device_id=(e, to_row, to_col), device_id_type=pl.DeviceIdType.MESH)
    for k in range(1, 4):
        pl.semaphore_signal(barrier, inc=1, device_id=((e + k) % 4, r, c), device_id_type=pl.DeviceIdType.MESH)

    pl.semaphore_wait(barrier, 21)

    def x_rows():
        return [
            remote(x_hbm.at[:, TILE - 1], xp.at[:, 0], xh_s, xh_r, down, c),
            remote(x_hbm.at[:, 0], xp.at[:, TILE + 1], xh_s, xh_r, up, c),
        ]

    def x_columns():
        copies = [
            remote(xe_ref.at[1], xcol.at[0], xh_s, xh_r, r, right),
            remote(xe_ref.at[0], xcol.at[1], xh_s, xh_r, r, left),
        ]
        for k, (to_row, to_col) in enumerate(corners):
            copies.append(remote(xc_ref.at[k], xcor.at[3 - k], xh_s, xh_r, to_row, to_col))
        return copies

    x_bytes = acc.at[0 : 4 * N_EX * TILE // 2 + 4 * N_EX]

    def g_halo(n):
        copies = [
            remote(gp.at[n, TILE], gp.at[n, 0], gh_s, gh_r.at[n], down, c),
            remote(gp.at[n, 1], gp.at[n, TILE + 1], gh_s, gh_r.at[n], up, c),
            remote(ge.at[1, n], gcol.at[0, n], gh_s, gh_r.at[n], r, right),
            remote(ge.at[0, n], gcol.at[1, n], gh_s, gh_r.at[n], r, left),
        ]
        for k, (to_row, to_col) in enumerate(corners):
            copies.append(remote(gc.at[k, n], gcor.at[3 - k, n], gh_s, gh_r.at[n], to_row, to_col))
        return copies

    def clear(pad, col, cor, n):
        count, at = (N_EX, slice(None)) if n is None else (1, pl.ds(n, 1))
        row_zero = jnp.zeros((count, 1, TILE, CH), BF16)
        col_zero = jnp.zeros((1, count, TILE, CH), BF16)
        cor_zero = jnp.zeros((1, N_EX, CH), F32) if n is None else jnp.zeros((1, 1, 16, CH), BF16)

        @pl.when(r == 0)
        def _():
            pad[at, 0:1] = row_zero
            cor[0:1, at] = cor_zero
            cor[1:2, at] = cor_zero

        @pl.when(r == 7)
        def _():
            pad[at, TILE + 1 : TILE + 2] = row_zero
            cor[2:3, at] = cor_zero
            cor[3:4, at] = cor_zero

        @pl.when(c == 0)
        def _():
            col[0:1, at] = col_zero
            cor[0:1, at] = cor_zero
            cor[2:3, at] = cor_zero

        @pl.when(c == 7)
        def _():
            col[1:2, at] = col_zero
            cor[1:2, at] = cor_zero
            cor[3:4, at] = cor_zero

    def spread(tap, pad, col, spot, n):
        tile = wide.reshape(TILE + 2, PITCH, CH)
        tile[:, 8 : 8 + TILE, :] = pad[n].astype(F32)
        for side, slot in ((0, 7), (1, 8 + TILE)):
            wide[pl.ds(PITCH + slot, TILE, stride=PITCH), :] = col[side, n].astype(F32)
            wide[slot : slot + 1, :] = spot(side)
            last = (TILE + 1) * PITCH + slot
            wide[last : last + 1, :] = spot(2 + side)
        tap[:, :, CH : 2 * CH] = pad[n]
        tap[:, :, 0:CH] = tile[:, 7 : 7 + TILE, :].astype(BF16)
        tap[:, :, 2 * CH :] = tile[:, 9 : 9 + TILE, :].astype(BF16)

    def conv(tap, weights):
        total = None
        for a in range(3):
            part = jnp.dot(
                tap[a : a + TILE].reshape(PIX, 3 * CH), weights[a], preferred_element_type=F32
            )
            total = part if total is None else total + part
        return total

    def core_copy(m):
        return remote(stage.at[m, 1 - core], crx.at[m], c_s, c_r.at[m], mate, c)

    def y1_copy(m):
        return remote(y1tx.at[m], y1rx.at[m], y1_s, y1_r.at[m], 2 * p1 + core, c)

    def y2_copy(m):
        return remote(y2tx.at[m], y2rx.at[m], y2_s, y2_r.at[m], 2 * p2 + core, c)

    def z_copy(m, k):
        to = (c + k) % 8
        return remote(zst.at[to, m], zrx.at[c, m], z_s, z_r, r, to)

    def step_y1(m):
        core_copy(m).wait_recv()

        def both(j):
            return stage[m, core, j].astype(F32) + crx[m, j].astype(F32)

        y1tx[m, 0] = both(p1).astype(BF16)
        y1tx[m, 1] = both(far).astype(BF16)
        y1_copy(m).start()
        y1own[m, 0] = both(y)
        y1own[m, 1] = both(p2)

    def step_y2(m):
        y1_copy(m).wait_recv()
        y2tx[m] = (y1own[m, 1] + y1rx[m, 1].astype(F32)).astype(BF16)
        y2_copy(m).start()
        y2own[m] = y1own[m, 0] + y1rx[m, 0].astype(F32)

    def step_z(m):
        y2_copy(m).wait_recv()
        t32[0:CHUNK, :] = y2own[m] + y2rx[m].astype(F32)
        for k in range(8):
            piece = t32[k * OWN : k * OWN + PIECE, :].astype(BF16)
            zst[k, m] = piece
        for k in range(1, 8):
            z_copy(m, k).start()
        zrx[c, m] = zst[c, m]

    for copy in x_rows():
        copy.start()

    def take_edges(n, carry):
        load_x(n).wait()
        for side in range(2):
            block = xp[n, 1 : TILE + 1, side * 16 : side * 16 + 16, :].astype(F32)
            edge[...] = block.reshape(TILE * 16, CH)
            column = edge[pl.ds(15 * side, TILE, stride=16), :]
            xe_ref[side, n] = column.astype(BF16)
            xc_ref[side, pl.ds(n, 1), :] = column[0:1]
            xc_ref[2 + side, pl.ds(n, 1), :] = column[TILE - 1 : TILE]
        return carry

    lax.fori_loop(0, N_EX, take_edges, 0)
    for copy in x_columns():
        copy.start()
    load_w.wait()
    load_b.wait()
    for a in range(3):
        for b in range(3):
            wback[2 - a, (2 - b) * CH : (3 - b) * CH, :] = w_ref[a, b * CH : (b + 1) * CH, :].T
    t32[...] = jnp.zeros_like(t32)
    received(x_bytes, xh_r)
    clear(xp, xcol, xcor, None)
    load_cot.wait()

    def forward(n):
        tap = taps.at[n % 2]
        spread(tap, xp, xcol, lambda k: xcor[k, pl.ds(n, 1), :], n)
        acc[...] = conv(tap, w_ref)

    def output_grad(n):
        half = 0.5 * (acc[...] + b_ref[...])
        t = jnp.tanh(half)
        slope = (1.0 + t) + half * (1.0 - t * t)
        g = (0.5 * cot[n].reshape(PIX, CH).astype(F32) * slope).astype(BF16)
        gp[n, 1 : TILE + 1] = g.reshape(TILE, TILE, CH)
        wide_g = g.astype(F32)
        g32[...] = wide_g
        bpart[n] = jnp.sum(wide_g.reshape(PIX // 8, 8, CH), axis=0)
        ge[0, n] = g32[pl.ds(0, TILE, stride=TILE), :].astype(BF16)
        ge[1, n] = g32[pl.ds(TILE - 1, TILE, stride=TILE), :].astype(BF16)
        for k, at in enumerate((0, TILE - 1, PIX - TILE, PIX - 1)):
            gc[k, n] = jnp.broadcast_to(g32[at : at + 1, :], (16, CH)).astype(BF16)

    def transpose_grad(n):
        gt[...] = gp[n, 1 : TILE + 1].reshape(PIX, CH).T

    def kernel_grad(n):
        tap = taps.at[n % 2]
        every = jnp.concatenate(
            [tap[a : a + TILE].reshape(PIX, 3 * CH) for a in range(3)], axis=1
        )
        for start in range(0, ROWS, 2 * CH):
            part = jnp.dot(gt[...], every[:, start : start + 2 * CH], preferred_element_type=F32)
            for b in range(part.shape[1] // CH):
                block = part[:, b * CH : (b + 1) * CH].T.astype(BF16)
                for k in range(8):
                    group = start // 16 + 8 * b + k
                    owner, at = group // 9, group % 9 * 16
                    stage[n, owner % 2, owner // 2, at : at + 16, :] = block[16 * k : 16 * k + 16]

    def first(n, carry):
        forward(n)
        kernel_grad(n - 1)
        output_grad(n)
        transpose_grad(n)
        for copy in g_halo(n):
            copy.start()
        core_copy(n - 1).start()

        @pl.when(n >= 2)
        def _():
            step_y1(n - 2)

        @pl.when(n >= 4)
        def _():
            step_y2(n - 4)

        @pl.when(n >= 6)
        def _():
            step_z(n - 6)

        return carry

    forward(0)
    output_grad(0)
    transpose_grad(0)
    for copy in g_halo(0):
        copy.start()
    lax.fori_loop(1, N_EX, first, 0)
    kernel_grad(N_EX - 1)
    core_copy(N_EX - 1).start()

    def b1_copy(k):
        return remote(b1st, b1rx.at[c], b1_s, b1_r, r, (c + k) % 8)

    def b2_copy(k):
        return remote(b2st, b2rx.at[r], b2_s, b2_r, (r + k) % 8, c)

    def n1_copy(k):
        return remote(n1st, n1rx.at[c], n1_s, n1_r, r, (c + k) % 8)

    def n2_copy(k):
        return remote(n2st, n2rx.at[r], n2_s, n2_r, (r + k) % 8, c)

    def e_copy(k):
        return remote(est, erx.at[e], e_s, e_r, r, c, (e + k) % 4)

    away = (4, 3, 5, 2, 6, 1, 7)

    def add_up(rx):
        total = rx[0]
        for k in range(1, 8):
            total = total + rx[k]
        return total

    def bias_z(_):
        for m in range(N_EX):
            b1st[m : m + 1, :] = jnp.sum(bpart[m], axis=0, keepdims=True)
        b1rx[c] = b1st[...]
        for k in away:
            b1_copy(k).start()

    def bias_row(_):
        received(b1rx.at[0:7], b1_r)
        total = add_up(b1rx)
        b2st[...] = total
        b2rx[r] = total
        for k in away:
            b2_copy(k).start()

    plan = {
        0: ((step_z, 2), (step_y2, 4), (step_y1, 6)),
        1: ((step_y1, 7), (bias_z, 0)),
        2: ((step_y2, 5), (step_z, 3)),
        3: ((step_z, 4),),
        4: ((step_y2, 6), (step_y2, 7)),
        5: ((step_z, 5), (bias_row, 0)),
        7: ((step_z, 6), (step_z, 7)),
    }

    def second(n, carry):
        received(gp.at[n, 0:6], gh_r.at[n])
        clear(gp, gcol, gcor, n)
        spread(taps.at[0], gp, gcol, lambda k: gcor[k, n].astype(F32)[0:1], n)
        out_ref[n] = conv(taps.at[0], wback).astype(BF16).reshape(TILE, TILE, CH)
        for when, steps in plan.items():

            @pl.when(n == when)
            def _(steps=steps):
                for step, m in steps:
                    step(m)

        return carry

    lax.fori_loop(0, N_EX, second, 0)

    received(b2rx.at[0:7], b2_r)
    bias_sum = add_up(b2rx)
    keep = lax.broadcasted_iota(jnp.int32, (8, CH), 0) < OWN - 16
    own_lane = lax.broadcasted_iota(jnp.int32, (8, CH), 1) // 16 == lax.broadcasted_iota(jnp.int32, (8, CH), 0)
    received(zrx.at[0:7], z_r)
    for m in range(N_EX):
        total = zrx[0, m].astype(F32)
        for k in range(1, 8):
            total = total + zrx[k, m].astype(F32)
        zacc[m] = total[0:24]
        square = total * total
        part = square[0:8] + square[8:16] + jnp.where(keep, square[16:24], 0.0)
        fst[m : m + 1, :] = jnp.sum(part, axis=0, keepdims=True)
    folded = fst[...]
    for width in (64, 32, 16):
        folded = folded + pltpu.roll(folded, width, 1)
    total = jnp.sum(jnp.where(own_lane, folded, 0.0), axis=0, keepdims=True)
    n1st[...] = total
    n1rx[c] = total
    for k in away:
        n1_copy(k).start()
    received(n1rx.at[0:7], n1_r)
    total = add_up(n1rx)
    n2st[...] = total
    n2rx[r] = total
    for k in away:
        n2_copy(k).start()
    received(n2rx.at[0:7], n2_r)
    total = add_up(n2rx)
    squares = jnp.where(own_lane, jnp.broadcast_to(total, (N_EX, CH)), 0.0) + bias_sum * bias_sum
    factor = jnp.minimum(1.0, clip / jnp.sqrt(jnp.sum(squares, axis=1, keepdims=True) + epsilon))
    fst[...] = jnp.broadcast_to(factor, (N_EX, CH))
    weighted = fst[0:1, :] * zacc[0]
    for m in range(1, N_EX):
        weighted = weighted + fst[m : m + 1, :] * zacc[m]
    est[...] = weighted
    est[OWN : OWN + 1, :] = jnp.sum(fst[...] * bias_sum, axis=0, keepdims=True)
    erx[e] = est[...]
    for k in (2, 1, 3):
        e_copy(k).start()
    received(erx.at[0:3], e_r)
    sum_ref[...] = (erx[0] + erx[1]) + (erx[2] + erx[3])

    sent(x_bytes, xh_s)
    sent(gp.at[:, 0:6], gh_s)
    sent(crx, c_s)
    sent(y1tx, y1_s)
    sent(y2tx, y2_s)
    sent(zst.at[0:7], z_s)
    sent(b1rx.at[0:7], b1_s)
    sent(b2rx.at[0:7], b2_s)
    sent(n1rx.at[0:7], n1_s)
    sent(n2rx.at[0:7], n2_s)
    sent(erx.at[0:3], e_s)


def local(inputs, cotangent, weight, bias, noise_weight, noise_bias):
    examples, tile_rows, tile_cols, channels = inputs.shape
    height = tile_rows * lax.axis_size("row")
    width = tile_cols * lax.axis_size("col")
    clip = math.sqrt(height * width * 9 * channels * channels)
    scale = 1.0 / math.sqrt(examples * lax.axis_size("ex") * height * width)
    vmem, hbm = pl.BlockSpec(memory_space=pltpu.VMEM), pl.BlockSpec(memory_space=pltpu.MemorySpace.HBM)
    halo_col, halo_cor = pltpu.VMEM((2, N_EX, TILE, CH), BF16), pltpu.VMEM((4, N_EX, 16, CH), BF16)
    spots = pltpu.VMEM((4, N_EX, CH), F32)
    dma = pltpu.SemaphoreType.DMA
    input_grad, total = pl.pallas_call(
        functools.partial(kernel, clip),
        out_shape=(
            jax.ShapeDtypeStruct(inputs.shape, BF16),
            jax.ShapeDtypeStruct((24, channels), F32),
        ),
        in_specs=[hbm] * 4,
        out_specs=[vmem, vmem],
        scratch_shapes=[
            pltpu.VMEM((3, 3 * CH, CH), BF16),
            pltpu.VMEM((1, CH), F32),
            halo_col, spots,
            pltpu.VMEM((TILE * 16, CH), F32),
            pltpu.VMEM((N_EX, TILE + 2, TILE, CH), BF16),
            pltpu.VMEM((N_EX, TILE, TILE, CH), BF16),
            pltpu.VMEM((N_EX, TILE + 2, TILE, CH), BF16),
            halo_col, spots, halo_col, halo_cor, halo_col, halo_cor,
            pltpu.VMEM(((TILE + 2) * PITCH, CH), F32),
            pltpu.VMEM((2, TILE + 2, TILE, 3 * CH), BF16),
            pltpu.VMEM((CH, PIX), BF16),
            pltpu.VMEM((PIX, CH), F32),
            pltpu.VMEM((3, 3 * CH, CH), BF16),
            pltpu.VMEM((PIX, CH), F32),
            pltpu.VMEM((N_EX, 2, 4, CHUNK, CH), BF16),
            pltpu.VMEM((N_EX, 4, CHUNK, CH), BF16),
            pltpu.VMEM((N_EX, 2, CHUNK, CH), F32),
            pltpu.VMEM((N_EX, 2, CHUNK, CH), BF16),
            pltpu.VMEM((N_EX, 2, CHUNK, CH), BF16),
            pltpu.VMEM((N_EX, CHUNK, CH), F32),
            pltpu.VMEM((N_EX, CHUNK, CH), BF16),
            pltpu.VMEM((N_EX, CHUNK, CH), BF16),
            pltpu.VMEM((CHUNK + 16, CH), F32),
            pltpu.VMEM((8, N_EX, PIECE, CH), BF16),
            pltpu.VMEM((8, N_EX, PIECE, CH), BF16),
            pltpu.VMEM((N_EX, 24, CH), F32),
            pltpu.VMEM((N_EX, 8, CH), F32),
            pltpu.VMEM((N_EX, CH), F32),
            pltpu.VMEM((8, N_EX, CH), F32),
            pltpu.VMEM((N_EX, CH), F32),
            pltpu.VMEM((8, N_EX, CH), F32),
            pltpu.VMEM((1, CH), F32),
            pltpu.VMEM((8, 1, CH), F32),
            pltpu.VMEM((1, CH), F32),
            pltpu.VMEM((8, 1, CH), F32),
            pltpu.VMEM((N_EX, CH), F32),
            pltpu.VMEM((24, CH), F32),
            pltpu.VMEM((4, 24, CH), F32),
            dma((2,)), dma((N_EX,)), dma(()),
            dma(()), dma(()), dma(()), dma((N_EX,)),
            dma(()), dma((N_EX,)), dma(()), dma((N_EX,)), dma(()), dma((N_EX,)), dma(()), dma(()),
            dma(()), dma(()), dma(()), dma(()), dma(()), dma(()), dma(()), dma(()), dma(()), dma(()),
        ],
        compiler_params=pltpu.CompilerParams(
            collective_id=0, has_side_effects=True, vmem_limit_bytes=48 * 2**20
        ),
        name="clipped_grad",
    )(
        *(
            pltpu.with_memory_space_constraint(operand, pltpu.MemorySpace.HBM)
            for operand in (
                inputs, cotangent, weight.reshape(3, 3 * channels, channels), bias.reshape(1, channels)
            )
        )
    )
    grad_weight = (total[0:OWN] + noise_multiplier * clip * noise_weight) * scale
    grad_bias = (total[OWN] + noise_multiplier * clip * noise_bias) * scale
    return input_grad, grad_weight, grad_bias


def solution(mesh):
    in_specs = (
        P("ex", "row", "col", None),
        P("ex", "row", "col", None),
        P(),
        P(),
        P(("row", "col"), None),
        P(),
    )
    out_specs = (P("ex", "row", "col", None), P(("row", "col"), None), P())
    return jax.shard_map(local, mesh=mesh, in_specs=in_specs, out_specs=out_specs, check_vma=False)
```

```python
import functools
import math

import jax
import jax.numpy as jnp
from jax import lax
from jax.experimental import pallas as pl
from jax.experimental.pallas import tpu as pltpu
from jax.sharding import PartitionSpec as P

noise_multiplier = 0.002
epsilon = 1e-06
F32 = jnp.float32
BF16 = jnp.bfloat16
N_EX = 8
TILE = 32
CH = 128
PITCH = 48
PIX = TILE * TILE
ROWS = 9 * CH
CHUNK = ROWS // 8
EARLY = 2
OWN = CHUNK // 8
PIECE = 32


def kernel(
    clip,
    x_hbm, cot_hbm, w_hbm, b_hbm,
    out_ref, sum_ref,
    w_ref, b_ref, xe_ref, xc_ref, edge, xp, cot, gp, xcol, xcor, gcol, gcor, ge, gc, wide, taps, gt, g32, wback, acc,
    stage, crx, y1own, y1tx, y1rx, y2own, y2tx, y2rx, t32, zst, zrx, zacc, bpart,
    b1st, b1rx, b2st, b2rx, n1st, n1rx, n2st, n2rx, fst, est, erx,
    lw_s, lx_s, lc_s, xh_s, xh_r, gh_s, gh_r, c_s, c_r, y1_s, y1_r, y2_s, y2_r, z_s, z_r,
    b1_s, b1_r, b2_s, b2_r, n1_s, n1_r, n2_s, n2_r, e_s, e_r,
):
    e, r, c = lax.axis_index("ex"), lax.axis_index("row"), lax.axis_index("col")
    core, y = r % 2, r // 2
    up, down, left, right = (r + 7) % 8, (r + 1) % 8, (c + 7) % 8, (c + 1) % 8
    mate = r + 1 - 2 * core
    flip, mirror = y + 1 - 2 * (y % 2), 3 - y
    p1 = flip + core * (mirror - flip)
    p2 = mirror + core * (flip - mirror)
    far = (y + 2) % 4
    corners = ((up, left), (up, right), (down, left), (down, right))

    def remote(src, dst, s_sem, r_sem, to_row, to_col, to_ex=None):
        return pltpu.make_async_remote_copy(
            src_ref=src, dst_ref=dst, send_sem=s_sem, recv_sem=r_sem,
            device_id=(e if to_ex is None else to_ex, to_row, to_col),
            device_id_type=pl.DeviceIdType.MESH,
        )

    def received(view, sem):
        remote(view, view, sem, sem, r, c).wait_recv()

    def sent(view, sem):
        remote(view, view, sem, sem, r, c).wait_send()

    def load_x(n):
        return pltpu.make_async_copy(x_hbm.at[n], xp.at[n, 1 : TILE + 1], lx_s.at[n])

    load_w = pltpu.make_async_copy(w_hbm, w_ref, lw_s.at[0])
    load_b = pltpu.make_async_copy(b_hbm, b_ref, lw_s.at[1])
    for n in range(N_EX):
        load_x(n).start()
    load_w.start()
    load_b.start()
    load_cot = pltpu.make_async_copy(cot_hbm, cot, lc_s)
    load_cot.start()

    barrier = pltpu.get_barrier_semaphore()
    partners = list(corners)
    partners += [((r + k) % 8, c) for k in range(1, 8)]
    partners += [(r, (c + k) % 8) for k in range(1, 8)]
    for to_row, to_col in partners:
        pl.semaphore_signal(barrier, inc=1, device_id=(e, to_row, to_col), device_id_type=pl.DeviceIdType.MESH)
    for k in range(1, 4):
        pl.semaphore_signal(barrier, inc=1, device_id=((e + k) % 4, r, c), device_id_type=pl.DeviceIdType.MESH)

    pl.semaphore_wait(barrier, 21)

    batches = ((0, EARLY), (EARLY, N_EX))

    def x_rows(k):
        some = pl.ds(batches[k][0], batches[k][1] - batches[k][0])
        return [
            remote(x_hbm.at[some, TILE - 1], xp.at[some, 0], xh_s, xh_r.at[k], down, c),
            remote(x_hbm.at[some, 0], xp.at[some, TILE + 1], xh_s, xh_r.at[k], up, c),
        ]

    def x_columns(k):
        some = pl.ds(batches[k][0], batches[k][1] - batches[k][0])
        copies = [
            remote(xe_ref.at[1, some], xcol.at[0, some], xh_s, xh_r.at[k], r, right),
            remote(xe_ref.at[0, some], xcol.at[1, some], xh_s, xh_r.at[k], r, left),
        ]
        for i, (to_row, to_col) in enumerate(corners):
            copies.append(remote(xc_ref.at[k, i], xcor.at[k, 3 - i], xh_s, xh_r.at[k], to_row, to_col))
        return copies

    def x_bytes(examples, parts):
        return acc.at[0 : 2 * TILE * examples + 4 * N_EX * parts]

    def g_halo(n):
        copies = [
            remote(gp.at[n, TILE], gp.at[n, 0], gh_s, gh_r.at[n], down, c),
            remote(gp.at[n, 1], gp.at[n, TILE + 1], gh_s, gh_r.at[n], up, c),
            remote(ge.at[1, n], gcol.at[0, n], gh_s, gh_r.at[n], r, right),
            remote(ge.at[0, n], gcol.at[1, n], gh_s, gh_r.at[n], r, left),
        ]
        for k, (to_row, to_col) in enumerate(corners):
            copies.append(remote(gc.at[k, n], gcor.at[3 - k, n], gh_s, gh_r.at[n], to_row, to_col))
        return copies

    def clear(pad, col, cor, at, count):
        row_zero = jnp.zeros((count, 1, TILE, CH), BF16)
        col_zero = jnp.zeros((1, count, TILE, CH), BF16)
        cor_zero = jnp.zeros(cor.shape[1:], cor.dtype)

        @pl.when(r == 0)
        def _():
            pad[at, 0:1] = row_zero
            cor[0] = cor_zero
            cor[1] = cor_zero

        @pl.when(r == 7)
        def _():
            pad[at, TILE + 1 : TILE + 2] = row_zero
            cor[2] = cor_zero
            cor[3] = cor_zero

        @pl.when(c == 0)
        def _():
            col[0:1, at] = col_zero
            cor[0] = cor_zero
            cor[2] = cor_zero

        @pl.when(c == 7)
        def _():
            col[1:2, at] = col_zero
            cor[1] = cor_zero
            cor[3] = cor_zero

    def clear_x(k):
        begin, end = batches[k]
        clear(xp, xcol, xcor.at[k], pl.ds(begin, end - begin), end - begin)

    def spread(tap, pad, col, spot, n):
        tile = wide.reshape(TILE + 2, PITCH, CH)
        tile[:, 8 : 8 + TILE, :] = pad[n].astype(F32)
        for side, slot in ((0, 7), (1, 8 + TILE)):
            wide[pl.ds(PITCH + slot, TILE, stride=PITCH), :] = col[side, n].astype(F32)
            wide[slot : slot + 1, :] = spot(side)
            last = (TILE + 1) * PITCH + slot
            wide[last : last + 1, :] = spot(2 + side)
        tap[:, :, CH : 2 * CH] = pad[n]
        tap[:, :, 0:CH] = tile[:, 7 : 7 + TILE, :].astype(BF16)
        tap[:, :, 2 * CH :] = tile[:, 9 : 9 + TILE, :].astype(BF16)

    def conv(tap, weights):
        total = None
        for a in range(3):
            part = jnp.dot(
                tap[a : a + TILE].reshape(PIX, 3 * CH), weights[a], preferred_element_type=F32
            )
            total = part if total is None else total + part
        return total

    def core_copy(m):
        return remote(stage.at[m, 1 - core], crx.at[m], c_s, c_r.at[m], mate, c)

    def y1_copy(m):
        return remote(y1tx.at[m], y1rx.at[m], y1_s, y1_r.at[m], 2 * p1 + core, c)

    def y2_copy(m):
        return remote(y2tx.at[m], y2rx.at[m], y2_s, y2_r.at[m], 2 * p2 + core, c)

    def z_copy(m, k):
        to = (c + k) % 8
        return remote(zst.at[to, m], zrx.at[c, m], z_s, z_r, r, to)

    def step_y1(m):
        core_copy(m).wait_recv()

        def both(j):
            return stage[m, core, j].astype(F32) + crx[m, j].astype(F32)

        y1tx[m, 0] = both(p1).astype(BF16)
        y1tx[m, 1] = both(far).astype(BF16)
        y1_copy(m).start()
        y1own[m, 0] = both(y)
        y1own[m, 1] = both(p2)

    def step_y2(m):
        y1_copy(m).wait_recv()
        y2tx[m] = (y1own[m, 1] + y1rx[m, 1].astype(F32)).astype(BF16)
        y2_copy(m).start()
        y2own[m] = y1own[m, 0] + y1rx[m, 0].astype(F32)

    def step_z(m):
        y2_copy(m).wait_recv()
        t32[0:CHUNK, :] = y2own[m] + y2rx[m].astype(F32)
        for k in range(8):
            piece = t32[k * OWN : k * OWN + PIECE, :].astype(BF16)
            zst[k, m] = piece
        for k in range(1, 8):
            z_copy(m, k).start()
        zrx[c, m] = zst[c, m]

    for k in range(2):
        for copy in x_rows(k):
            copy.start()

    def take_edges(k, n):
        load_x(n).wait()
        for side in range(2):
            block = xp[n, 1 : TILE + 1, side * 16 : side * 16 + 16, :].astype(F32)
            edge[...] = block.reshape(TILE * 16, CH)
            column = edge[pl.ds(15 * side, TILE, stride=16), :]
            xe_ref[side, n] = column.astype(BF16)
            xc_ref[k, side, pl.ds(n, 1), :] = column[0:1]
            xc_ref[k, 2 + side, pl.ds(n, 1), :] = column[TILE - 1 : TILE]

    xc_ref[...] = jnp.zeros_like(xc_ref)
    for k, (begin, end) in enumerate(batches):
        lax.fori_loop(begin, end, lambda n, carry, k=k: (take_edges(k, n), carry)[1], 0)
        for copy in x_columns(k):
            copy.start()
    load_w.wait()
    load_b.wait()
    for a in range(3):
        for b in range(3):
            wback[2 - a, (2 - b) * CH : (3 - b) * CH, :] = w_ref[a, b * CH : (b + 1) * CH, :].T
    t32[...] = jnp.zeros_like(t32)
    load_cot.wait()
    received(x_bytes(EARLY, 1), xh_r.at[0])
    clear_x(0)

    def forward(n):
        tap = taps.at[n % 2]
        batch = 0 if isinstance(n, int) else (n + N_EX - EARLY) // N_EX
        spread(tap, xp, xcol, lambda k: xcor[batch, k, pl.ds(n, 1), :], n)
        acc[...] = conv(tap, w_ref)

    def output_grad(n):
        half = 0.5 * (acc[...] + b_ref[...])
        t = jnp.tanh(half)
        slope = (1.0 + t) + half * (1.0 - t * t)
        g = (0.5 * cot[n].reshape(PIX, CH).astype(F32) * slope).astype(BF16)
        gp[n, 1 : TILE + 1] = g.reshape(TILE, TILE, CH)
        wide_g = g.astype(F32)
        g32[...] = wide_g
        bpart[n] = jnp.sum(wide_g.reshape(PIX // 8, 8, CH), axis=0)
        ge[0, n] = g32[pl.ds(0, TILE, stride=TILE), :].astype(BF16)
        ge[1, n] = g32[pl.ds(TILE - 1, TILE, stride=TILE), :].astype(BF16)
        for k, at in enumerate((0, TILE - 1, PIX - TILE, PIX - 1)):
            gc[k, n] = jnp.broadcast_to(g32[at : at + 1, :], (16, CH)).astype(BF16)

    def transpose_grad(n):
        gt[...] = gp[n, 1 : TILE + 1].reshape(PIX, CH).T

    def kernel_grad(n):
        tap = taps.at[n % 2]
        every = jnp.concatenate(
            [tap[a : a + TILE].reshape(PIX, 3 * CH) for a in range(3)], axis=1
        )
        for start in range(0, ROWS, 2 * CH):
            part = jnp.dot(gt[...], every[:, start : start + 2 * CH], preferred_element_type=F32)
            for b in range(part.shape[1] // CH):
                block = part[:, b * CH : (b + 1) * CH].T.astype(BF16)
                for k in range(8):
                    group = start // 16 + 8 * b + k
                    owner, at = group // 9, group % 9 * 16
                    stage[n, owner % 2, owner // 2, at : at + 16, :] = block[16 * k : 16 * k + 16]

    def first(n, carry):
        @pl.when(n == EARLY)
        def _():
            received(x_bytes(N_EX - EARLY, 1), xh_r.at[1])
            clear_x(1)

        forward(n)
        kernel_grad(n - 1)
        output_grad(n)
        transpose_grad(n)
        for copy in g_halo(n):
            copy.start()
        core_copy(n - 1).start()

        @pl.when(n >= 2)
        def _():
            step_y1(n - 2)

        @pl.when(n >= 4)
        def _():
            step_y2(n - 4)

        @pl.when(n >= 6)
        def _():
            step_z(n - 6)

        return carry

    forward(0)
    output_grad(0)
    transpose_grad(0)
    for copy in g_halo(0):
        copy.start()
    lax.fori_loop(1, N_EX, first, 0)
    kernel_grad(N_EX - 1)
    core_copy(N_EX - 1).start()

    def b1_copy(k):
        return remote(b1st, b1rx.at[c], b1_s, b1_r, r, (c + k) % 8)

    def b2_copy(k):
        return remote(b2st, b2rx.at[r], b2_s, b2_r, (r + k) % 8, c)

    def n1_copy(k):
        return remote(n1st, n1rx.at[c], n1_s, n1_r, r, (c + k) % 8)

    def n2_copy(k):
        return remote(n2st, n2rx.at[r], n2_s, n2_r, (r + k) % 8, c)

    def e_copy(k):
        return remote(est, erx.at[e], e_s, e_r, r, c, (e + k) % 4)

    away = (4, 3, 5, 2, 6, 1, 7)

    def add_up(rx):
        total = rx[0]
        for k in range(1, 8):
            total = total + rx[k]
        return total

    def bias_z(_):
        for m in range(N_EX):
            b1st[m : m + 1, :] = jnp.sum(bpart[m], axis=0, keepdims=True)
        b1rx[c] = b1st[...]
        for k in away:
            b1_copy(k).start()

    def bias_row(_):
        received(b1rx.at[0:7], b1_r)
        total = add_up(b1rx)
        b2st[...] = total
        b2rx[r] = total
        for k in away:
            b2_copy(k).start()

    plan = {
        0: ((step_z, 2), (step_y2, 4), (step_y1, 6)),
        1: ((step_y1, 7), (bias_z, 0)),
        2: ((step_y2, 5), (step_z, 3)),
        3: ((step_z, 4),),
        4: ((step_y2, 6), (step_y2, 7)),
        5: ((step_z, 5), (bias_row, 0)),
        7: ((step_z, 6), (step_z, 7)),
    }

    def second(n, carry):
        received(gp.at[n, 0:6], gh_r.at[n])
        clear(gp, gcol, gcor.at[:, n], pl.ds(n, 1), 1)
        spread(taps.at[0], gp, gcol, lambda k: gcor[k, n].astype(F32)[0:1], n)
        out_ref[n] = conv(taps.at[0], wback).astype(BF16).reshape(TILE, TILE, CH)
        for when, steps in plan.items():

            @pl.when(n == when)
            def _(steps=steps):
                for step, m in steps:
                    step(m)

        return carry

    lax.fori_loop(0, N_EX, second, 0)

    received(b2rx.at[0:7], b2_r)
    bias_sum = add_up(b2rx)
    keep = lax.broadcasted_iota(jnp.int32, (8, CH), 0) < OWN - 16
    own_lane = lax.broadcasted_iota(jnp.int32, (8, CH), 1) // 16 == lax.broadcasted_iota(jnp.int32, (8, CH), 0)
    received(zrx.at[0:7], z_r)
    for m in range(N_EX):
        total = zrx[0, m].astype(F32)
        for k in range(1, 8):
            total = total + zrx[k, m].astype(F32)
        zacc[m] = total[0:24]
        square = total * total
        part = square[0:8] + square[8:16] + jnp.where(keep, square[16:24], 0.0)
        fst[m : m + 1, :] = jnp.sum(part, axis=0, keepdims=True)
    folded = fst[...]
    for width in (64, 32, 16):
        folded = folded + pltpu.roll(folded, width, 1)
    total = jnp.sum(jnp.where(own_lane, folded, 0.0), axis=0, keepdims=True)
    n1st[...] = total
    n1rx[c] = total
    for k in away:
        n1_copy(k).start()
    received(n1rx.at[0:7], n1_r)
    total = add_up(n1rx)
    n2st[...] = total
    n2rx[r] = total
    for k in away:
        n2_copy(k).start()
    received(n2rx.at[0:7], n2_r)
    total = add_up(n2rx)
    squares = jnp.where(own_lane, jnp.broadcast_to(total, (N_EX, CH)), 0.0) + bias_sum * bias_sum
    factor = jnp.minimum(1.0, clip / jnp.sqrt(jnp.sum(squares, axis=1, keepdims=True) + epsilon))
    fst[...] = jnp.broadcast_to(factor, (N_EX, CH))
    weighted = fst[0:1, :] * zacc[0]
    for m in range(1, N_EX):
        weighted = weighted + fst[m : m + 1, :] * zacc[m]
    est[...] = weighted
    est[OWN : OWN + 1, :] = jnp.sum(fst[...] * bias_sum, axis=0, keepdims=True)
    erx[e] = est[...]
    for k in (2, 1, 3):
        e_copy(k).start()
    received(erx.at[0:3], e_r)
    sum_ref[...] = (erx[0] + erx[1]) + (erx[2] + erx[3])

    sent(x_bytes(N_EX, 2), xh_s)
    sent(gp.at[:, 0:6], gh_s)
    sent(crx, c_s)
    sent(y1tx, y1_s)
    sent(y2tx, y2_s)
    sent(zst.at[0:7], z_s)
    sent(b1rx.at[0:7], b1_s)
    sent(b2rx.at[0:7], b2_s)
    sent(n1rx.at[0:7], n1_s)
    sent(n2rx.at[0:7], n2_s)
    sent(erx.at[0:3], e_s)


def finish(clip, scale, grad_ref, sum_ref, nw_ref, nb_ref, out_hbm, gw_ref, gb_ref, sem):
    store = pltpu.make_async_copy(grad_ref, out_hbm, sem)
    store.start()
    gw_ref[...] = (sum_ref[0:OWN] + noise_multiplier * clip * nw_ref[...]) * scale
    gb_ref[...] = (sum_ref[OWN : OWN + 1] + noise_multiplier * clip * nb_ref[...]) * scale
    store.wait()


def local(inputs, cotangent, weight, bias, noise_weight, noise_bias):
    examples, tile_rows, tile_cols, channels = inputs.shape
    height = tile_rows * lax.axis_size("row")
    width = tile_cols * lax.axis_size("col")
    clip = math.sqrt(height * width * 9 * channels * channels)
    scale = 1.0 / math.sqrt(examples * lax.axis_size("ex") * height * width)
    vmem, hbm = pl.BlockSpec(memory_space=pltpu.VMEM), pl.BlockSpec(memory_space=pltpu.MemorySpace.HBM)
    halo_col, halo_cor = pltpu.VMEM((2, N_EX, TILE, CH), BF16), pltpu.VMEM((4, N_EX, 16, CH), BF16)
    spots = pltpu.VMEM((2, 4, N_EX, CH), F32)
    dma = pltpu.SemaphoreType.DMA
    input_grad, total = pl.pallas_call(
        functools.partial(kernel, clip),
        out_shape=(
            jax.ShapeDtypeStruct(inputs.shape, BF16),
            jax.ShapeDtypeStruct((24, channels), F32),
        ),
        in_specs=[hbm] * 4,
        out_specs=[vmem, vmem],
        scratch_shapes=[
            pltpu.VMEM((3, 3 * CH, CH), BF16),
            pltpu.VMEM((1, CH), F32),
            halo_col, spots,
            pltpu.VMEM((TILE * 16, CH), F32),
            pltpu.VMEM((N_EX, TILE + 2, TILE, CH), BF16),
            pltpu.VMEM((N_EX, TILE, TILE, CH), BF16),
            pltpu.VMEM((N_EX, TILE + 2, TILE, CH), BF16),
            halo_col, spots, halo_col, halo_cor, halo_col, halo_cor,
            pltpu.VMEM(((TILE + 2) * PITCH, CH), F32),
            pltpu.VMEM((2, TILE + 2, TILE, 3 * CH), BF16),
            pltpu.VMEM((CH, PIX), BF16),
            pltpu.VMEM((PIX, CH), F32),
            pltpu.VMEM((3, 3 * CH, CH), BF16),
            pltpu.VMEM((PIX, CH), F32),
            pltpu.VMEM((N_EX, 2, 4, CHUNK, CH), BF16),
            pltpu.VMEM((N_EX, 4, CHUNK, CH), BF16),
            pltpu.VMEM((N_EX, 2, CHUNK, CH), F32),
            pltpu.VMEM((N_EX, 2, CHUNK, CH), BF16),
            pltpu.VMEM((N_EX, 2, CHUNK, CH), BF16),
            pltpu.VMEM((N_EX, CHUNK, CH), F32),
            pltpu.VMEM((N_EX, CHUNK, CH), BF16),
            pltpu.VMEM((N_EX, CHUNK, CH), BF16),
            pltpu.VMEM((CHUNK + 16, CH), F32),
            pltpu.VMEM((8, N_EX, PIECE, CH), BF16),
            pltpu.VMEM((8, N_EX, PIECE, CH), BF16),
            pltpu.VMEM((N_EX, 24, CH), F32),
            pltpu.VMEM((N_EX, 8, CH), F32),
            pltpu.VMEM((N_EX, CH), F32),
            pltpu.VMEM((8, N_EX, CH), F32),
            pltpu.VMEM((N_EX, CH), F32),
            pltpu.VMEM((8, N_EX, CH), F32),
            pltpu.VMEM((1, CH), F32),
            pltpu.VMEM((8, 1, CH), F32),
            pltpu.VMEM((1, CH), F32),
            pltpu.VMEM((8, 1, CH), F32),
            pltpu.VMEM((N_EX, CH), F32),
            pltpu.VMEM((24, CH), F32),
            pltpu.VMEM((4, 24, CH), F32),
            dma((2,)), dma((N_EX,)), dma(()),
            dma(()), dma((2,)), dma(()), dma((N_EX,)),
            dma(()), dma((N_EX,)), dma(()), dma((N_EX,)), dma(()), dma((N_EX,)), dma(()), dma(()),
            dma(()), dma(()), dma(()), dma(()), dma(()), dma(()), dma(()), dma(()), dma(()), dma(()),
        ],
        compiler_params=pltpu.CompilerParams(
            collective_id=0, has_side_effects=True, vmem_limit_bytes=48 * 2**20
        ),
        name="clipped_grad",
    )(
        *(
            pltpu.with_memory_space_constraint(operand, pltpu.MemorySpace.HBM)
            for operand in (
                inputs, cotangent, weight.reshape(3, 3 * channels, channels), bias.reshape(1, channels)
            )
        )
    )
    input_grad, grad_weight, grad_bias = pl.pallas_call(
        functools.partial(finish, clip, scale),
        out_shape=(
            jax.ShapeDtypeStruct(inputs.shape, BF16),
            jax.ShapeDtypeStruct(noise_weight.shape, F32),
            jax.ShapeDtypeStruct((1, channels), F32),
        ),
        in_specs=[vmem] * 4,
        out_specs=[hbm, vmem, vmem],
        scratch_shapes=[dma(())],
        compiler_params=pltpu.CompilerParams(vmem_limit_bytes=16 * 2**20),
        name="finish",
    )(input_grad, total, noise_weight, noise_bias.reshape(1, channels))
    return input_grad, grad_weight, grad_bias.reshape(channels)


def solution(mesh):
    in_specs = (
        P("ex", "row", "col", None),
        P("ex", "row", "col", None),
        P(),
        P(),
        P(("row", "col"), None),
        P(),
    )
    out_specs = (P("ex", "row", "col", None), P(("row", "col"), None), P())
    return jax.shard_map(local, mesh=mesh, in_specs=in_specs, out_specs=out_specs, check_vma=False)
```

```python
import functools
import math

import jax
import jax.numpy as jnp
from jax import lax
from jax.experimental import pallas as pl
from jax.experimental.pallas import tpu as pltpu
from jax.sharding import PartitionSpec as P

noise_multiplier = 0.002
epsilon = 1e-06
F32 = jnp.float32
BF16 = jnp.bfloat16
N_EX = 8
TILE = 32
CH = 128
PITCH = 48
PIX = TILE * TILE
ROWS = 9 * CH
CHUNK = ROWS // 8
EARLY = 2
OWN = CHUNK // 8
PIECE = 32


def kernel(
    clip,
    x_hbm, cot_hbm, w_hbm, b_hbm,
    out_ref, sum_ref,
    w_ref, b_ref, xe_ref, xc_ref, edge, xp, cot, gp, xcol, xcor, gcol, gcor, ge, gc, wide, taps, gt, g32, wback, acc,
    stage, crx, y1own, y1tx, y1rx, y2own, y2tx, y2rx, t32, zst, zrx, zacc, bpart,
    b1st, b1rx, b2st, b2rx, n1st, n1rx, n2st, n2rx, fst, est, erx,
    lw_s, lx_s, lc_s, xh_s, xh_r, gh_s, gh_r, c_s, c_r, y1_s, y1_r, y2_s, y2_r, z_s, z_r,
    b1_s, b1_r, b2_s, b2_r, n1_s, n1_r, n2_s, n2_r, e_s, e_r,
):
    e, r, c = lax.axis_index("ex"), lax.axis_index("row"), lax.axis_index("col")
    core, y = r % 2, r // 2
    up, down, left, right = (r + 7) % 8, (r + 1) % 8, (c + 7) % 8, (c + 1) % 8
    mate = r + 1 - 2 * core
    flip, mirror = y + 1 - 2 * (y % 2), 3 - y
    p1 = flip + core * (mirror - flip)
    p2 = mirror + core * (flip - mirror)
    far = (y + 2) % 4
    corners = ((up, left), (up, right), (down, left), (down, right))

    def remote(src, dst, s_sem, r_sem, to_row, to_col, to_ex=None):
        return pltpu.make_async_remote_copy(
            src_ref=src, dst_ref=dst, send_sem=s_sem, recv_sem=r_sem,
            device_id=(e if to_ex is None else to_ex, to_row, to_col),
            device_id_type=pl.DeviceIdType.MESH,
        )

    def received(view, sem):
        remote(view, view, sem, sem, r, c).wait_recv()

    def sent(view, sem):
        remote(view, view, sem, sem, r, c).wait_send()

    def load_x(n):
        return pltpu.make_async_copy(x_hbm.at[n], xp.at[n, 1 : TILE + 1], lx_s.at[n])

    barrier = pltpu.get_barrier_semaphore()
    partners = list(corners)
    partners += [((r + k) % 8, c) for k in range(1, 8)]
    partners += [(r, (c + k) % 8) for k in range(1, 8)]
    for to_row, to_col in partners:
        pl.semaphore_signal(barrier, inc=1, device_id=(e, to_row, to_col), device_id_type=pl.DeviceIdType.MESH)
    for k in range(1, 4):
        pl.semaphore_signal(barrier, inc=1, device_id=((e + k) % 4, r, c), device_id_type=pl.DeviceIdType.MESH)

    load_w = pltpu.make_async_copy(w_hbm, w_ref, lw_s.at[0])
    load_b = pltpu.make_async_copy(b_hbm, b_ref, lw_s.at[1])
    for n in range(N_EX):
        load_x(n).start()
    load_w.start()
    load_b.start()
    load_cot = pltpu.make_async_copy(cot_hbm, cot, lc_s)
    load_cot.start()

    pl.semaphore_wait(barrier, 21)

    batches = ((0, EARLY), (EARLY, N_EX))

    def x_rows(k):
        some = pl.ds(batches[k][0], batches[k][1] - batches[k][0])
        return [
            remote(x_hbm.at[some, TILE - 1], xp.at[some, 0], xh_s, xh_r.at[k], down, c),
            remote(x_hbm.at[some, 0], xp.at[some, TILE + 1], xh_s, xh_r.at[k], up, c),
        ]

    def x_columns(k):
        some = pl.ds(batches[k][0], batches[k][1] - batches[k][0])
        copies = [
            remote(xe_ref.at[1, some], xcol.at[0, some], xh_s, xh_r.at[k], r, right),
            remote(xe_ref.at[0, some], xcol.at[1, some], xh_s, xh_r.at[k], r, left),
        ]
        for i, (to_row, to_col) in enumerate(corners):
            copies.append(remote(xc_ref.at[k, i], xcor.at[k, 3 - i], xh_s, xh_r.at[k], to_row, to_col))
        return copies

    def x_bytes(examples, parts):
        return acc.at[0 : 2 * TILE * examples + 4 * N_EX * parts]

    def g_halo(n):
        copies = [
            remote(gp.at[n, TILE], gp.at[n, 0], gh_s, gh_r.at[n], down, c),
            remote(gp.at[n, 1], gp.at[n, TILE + 1], gh_s, gh_r.at[n], up, c),
            remote(ge.at[1, n], gcol.at[0, n], gh_s, gh_r.at[n], r, right),
            remote(ge.at[0, n], gcol.at[1, n], gh_s, gh_r.at[n], r, left),
        ]
        for k, (to_row, to_col) in enumerate(corners):
            copies.append(remote(gc.at[k, n], gcor.at[3 - k, n], gh_s, gh_r.at[n], to_row, to_col))
        return copies

    def clear(pad, col, cor, at, count):
        row_zero = jnp.zeros((count, 1, TILE, CH), BF16)
        col_zero = jnp.zeros((1, count, TILE, CH), BF16)
        cor_zero = jnp.zeros(cor.shape[1:], cor.dtype)

        @pl.when(r == 0)
        def _():
            pad[at, 0:1] = row_zero
            cor[0] = cor_zero
            cor[1] = cor_zero

        @pl.when(r == 7)
        def _():
            pad[at, TILE + 1 : TILE + 2] = row_zero
            cor[2] = cor_zero
            cor[3] = cor_zero

        @pl.when(c == 0)
        def _():
            col[0:1, at] = col_zero
            cor[0] = cor_zero
            cor[2] = cor_zero

        @pl.when(c == 7)
        def _():
            col[1:2, at] = col_zero
            cor[1] = cor_zero
            cor[3] = cor_zero

    def clear_x(k):
        begin, end = batches[k]
        clear(xp, xcol, xcor.at[k], pl.ds(begin, end - begin), end - begin)

    def spread(tap, pad, col, spot, n):
        tile = wide.reshape(TILE + 2, PITCH, CH)
        tile[:, 8 : 8 + TILE, :] = pad[n].astype(F32)
        for side, slot in ((0, 7), (1, 8 + TILE)):
            wide[pl.ds(PITCH + slot, TILE, stride=PITCH), :] = col[side, n].astype(F32)
            wide[slot : slot + 1, :] = spot(side)
            last = (TILE + 1) * PITCH + slot
            wide[last : last + 1, :] = spot(2 + side)
        tap[:, :, CH : 2 * CH] = pad[n]
        tap[:, :, 0:CH] = tile[:, 7 : 7 + TILE, :].astype(BF16)
        tap[:, :, 2 * CH :] = tile[:, 9 : 9 + TILE, :].astype(BF16)

    def conv(tap, weights):
        total = None
        for a in range(3):
            part = jnp.dot(
                tap[a : a + TILE].reshape(PIX, 3 * CH), weights[a], preferred_element_type=F32
            )
            total = part if total is None else total + part
        return total

    def core_copy(m):
        return remote(stage.at[m, 1 - core], crx.at[m], c_s, c_r.at[m], mate, c)

    def y1_copy(m):
        return remote(y1tx.at[m], y1rx.at[m], y1_s, y1_r.at[m], 2 * p1 + core, c)

    def y2_copy(m):
        return remote(y2tx.at[m], y2rx.at[m], y2_s, y2_r.at[m], 2 * p2 + core, c)

    def z_copy(m, k):
        to = (c + k) % 8
        return remote(zst.at[to, m], zrx.at[c, m], z_s, z_r, r, to)

    def step_y1(m):
        core_copy(m).wait_recv()

        def both(j):
            return stage[m, core, j].astype(F32) + crx[m, j].astype(F32)

        y1tx[m, 0] = both(p1).astype(BF16)
        y1tx[m, 1] = both(far).astype(BF16)
        y1_copy(m).start()
        y1own[m, 0] = both(y)
        y1own[m, 1] = both(p2)

    def step_y2(m):
        y1_copy(m).wait_recv()
        y2tx[m] = (y1own[m, 1] + y1rx[m, 1].astype(F32)).astype(BF16)
        y2_copy(m).start()
        y2own[m] = y1own[m, 0] + y1rx[m, 0].astype(F32)

    def step_z(m):
        y2_copy(m).wait_recv()
        t32[0:CHUNK, :] = y2own[m] + y2rx[m].astype(F32)
        for k in range(8):
            piece = t32[k * OWN : k * OWN + PIECE, :].astype(BF16)
            zst[k, m] = piece
        for k in (4, 3, 5, 2, 6, 1, 7):
            z_copy(m, k).start()
        zrx[c, m] = zst[c, m]

    for k in range(2):
        for copy in x_rows(k):
            copy.start()

    def take_edges(k, n):
        load_x(n).wait()
        for side in range(2):
            block = xp[n, 1 : TILE + 1, side * 16 : side * 16 + 16, :].astype(F32)
            edge[...] = block.reshape(TILE * 16, CH)
            column = edge[pl.ds(15 * side, TILE, stride=16), :]
            xe_ref[side, n] = column.astype(BF16)
            xc_ref[k, side, pl.ds(n, 1), :] = column[0:1]
            xc_ref[k, 2 + side, pl.ds(n, 1), :] = column[TILE - 1 : TILE]

    xc_ref[...] = jnp.zeros_like(xc_ref)
    for k, (begin, end) in enumerate(batches):
        lax.fori_loop(begin, end, lambda n, carry, k=k: (take_edges(k, n), carry)[1], 0)
        for copy in x_columns(k):
            copy.start()
    load_w.wait()
    load_b.wait()
    for a in range(3):
        for b in range(3):
            wback[2 - a, (2 - b) * CH : (3 - b) * CH, :] = w_ref[a, b * CH : (b + 1) * CH, :].T
    t32[...] = jnp.zeros_like(t32)
    load_cot.wait()
    received(x_bytes(EARLY, 1), xh_r.at[0])
    clear_x(0)

    def forward(n):
        tap = taps.at[n % 2]
        batch = 0 if isinstance(n, int) else (n + N_EX - EARLY) // N_EX
        spread(tap, xp, xcol, lambda k: xcor[batch, k, pl.ds(n, 1), :], n)
        acc[...] = conv(tap, w_ref)

    def output_grad(n):
        half = 0.5 * (acc[...] + b_ref[...])
        t = jnp.tanh(half)
        slope = (1.0 + t) + half * (1.0 - t * t)
        g = (0.5 * cot[n].reshape(PIX, CH).astype(F32) * slope).astype(BF16)
        gp[n, 1 : TILE + 1] = g.reshape(TILE, TILE, CH)
        wide_g = g.astype(F32)
        g32[...] = wide_g
        bpart[n] = jnp.sum(wide_g.reshape(PIX // 8, 8, CH), axis=0)
        ge[0, n] = g32[pl.ds(0, TILE, stride=TILE), :].astype(BF16)
        ge[1, n] = g32[pl.ds(TILE - 1, TILE, stride=TILE), :].astype(BF16)
        for k, at in enumerate((0, TILE - 1, PIX - TILE, PIX - 1)):
            gc[k, n] = jnp.broadcast_to(g32[at : at + 1, :], (16, CH)).astype(BF16)

    def transpose_grad(n):
        gt[...] = gp[n, 1 : TILE + 1].reshape(PIX, CH).T

    def kernel_grad(n):
        tap = taps.at[n % 2]
        every = jnp.concatenate(
            [tap[a : a + TILE].reshape(PIX, 3 * CH) for a in range(3)], axis=1
        )
        for start in range(0, ROWS, 2 * CH):
            part = jnp.dot(gt[...], every[:, start : start + 2 * CH], preferred_element_type=F32)
            for b in range(part.shape[1] // CH):
                block = part[:, b * CH : (b + 1) * CH].T.astype(BF16)
                for k in range(8):
                    group = start // 16 + 8 * b + k
                    owner, at = group // 9, group % 9 * 16
                    stage[n, owner % 2, owner // 2, at : at + 16, :] = block[16 * k : 16 * k + 16]

    def first(n, carry):
        @pl.when(n == EARLY)
        def _():
            received(x_bytes(N_EX - EARLY, 1), xh_r.at[1])
            clear_x(1)

        forward(n)
        kernel_grad(n - 1)
        output_grad(n)
        transpose_grad(n)
        for copy in g_halo(n):
            copy.start()
        core_copy(n - 1).start()

        @pl.when(n >= 2)
        def _():
            step_y1(n - 2)

        @pl.when(n >= 4)
        def _():
            step_y2(n - 4)

        @pl.when(n >= 6)
        def _():
            step_z(n - 6)

        return carry

    forward(0)
    output_grad(0)
    transpose_grad(0)
    for copy in g_halo(0):
        copy.start()
    lax.fori_loop(1, N_EX, first, 0)
    kernel_grad(N_EX - 1)
    core_copy(N_EX - 1).start()

    def b1_copy(k):
        return remote(b1st, b1rx.at[c], b1_s, b1_r, r, (c + k) % 8)

    def b2_copy(k):
        return remote(b2st, b2rx.at[r], b2_s, b2_r, (r + k) % 8, c)

    def n1_copy(k):
        return remote(n1st, n1rx.at[c], n1_s, n1_r, r, (c + k) % 8)

    def n2_copy(k):
        return remote(n2st, n2rx.at[r], n2_s, n2_r, (r + k) % 8, c)

    def e_copy(k):
        return remote(est, erx.at[e], e_s, e_r, r, c, (e + k) % 4)

    away = (4, 3, 5, 2, 6, 1, 7)

    def add_up(rx):
        total = rx[0]
        for k in range(1, 8):
            total = total + rx[k]
        return total

    def bias_z(_):
        for m in range(N_EX):
            b1st[m : m + 1, :] = jnp.sum(bpart[m], axis=0, keepdims=True)
        b1rx[c] = b1st[...]
        for k in away:
            b1_copy(k).start()

    def bias_row(_):
        received(b1rx.at[0:7], b1_r)
        total = add_up(b1rx)
        b2st[...] = total
        b2rx[r] = total
        for k in away:
            b2_copy(k).start()

    plan = {
        0: ((step_z, 2), (step_y2, 4), (step_y1, 6), (bias_z, 0),),
        1: ((step_y1, 7), (step_z, 3),),
        2: ((step_y2, 5),),
        3: ((step_y2, 6), (step_z, 4),),
        4: ((step_y2, 7),),
        5: ((step_z, 5),),
        6: ((step_z, 6),),
        7: ((step_z, 7), (bias_row, 0),),
    }

    def second(n, carry):
        received(gp.at[n, 0:6], gh_r.at[n])
        clear(gp, gcol, gcor.at[:, n], pl.ds(n, 1), 1)
        spread(taps.at[0], gp, gcol, lambda k: gcor[k, n].astype(F32)[0:1], n)
        out_ref[n] = conv(taps.at[0], wback).astype(BF16).reshape(TILE, TILE, CH)
        for when, steps in plan.items():

            @pl.when(n == when)
            def _(steps=steps):
                for step, m in steps:
                    step(m)

        return carry

    lax.fori_loop(0, N_EX, second, 0)

    keep = lax.broadcasted_iota(jnp.int32, (8, CH), 0) < OWN - 16
    own_lane = lax.broadcasted_iota(jnp.int32, (8, CH), 1) // 16 == lax.broadcasted_iota(jnp.int32, (8, CH), 0)
    received(zrx.at[0:7], z_r)
    for m in range(N_EX):
        total = zrx[0, m].astype(F32)
        for k in range(1, 8):
            total = total + zrx[k, m].astype(F32)
        zacc[m] = total[0:24]
        square = total * total
        part = square[0:8] + square[8:16] + jnp.where(keep, square[16:24], 0.0)
        fst[m : m + 1, :] = jnp.sum(part, axis=0, keepdims=True)
    folded = fst[...]
    for width in (64, 32, 16):
        folded = folded + pltpu.roll(folded, width, 1)
    total = jnp.sum(jnp.where(own_lane, folded, 0.0), axis=0, keepdims=True)
    n1st[...] = total
    n1rx[c] = total
    for k in away:
        n1_copy(k).start()
    received(b2rx.at[0:7], b2_r)
    bias_sum = add_up(b2rx)
    received(n1rx.at[0:7], n1_r)
    total = add_up(n1rx)
    n2st[...] = total
    n2rx[r] = total
    for k in away:
        n2_copy(k).start()
    received(n2rx.at[0:7], n2_r)
    total = add_up(n2rx)
    squares = jnp.where(own_lane, jnp.broadcast_to(total, (N_EX, CH)), 0.0) + bias_sum * bias_sum
    factor = jnp.minimum(1.0, clip / jnp.sqrt(jnp.sum(squares, axis=1, keepdims=True) + epsilon))
    fst[...] = jnp.broadcast_to(factor, (N_EX, CH))
    weighted = fst[0:1, :] * zacc[0]
    for m in range(1, N_EX):
        weighted = weighted + fst[m : m + 1, :] * zacc[m]
    est[...] = weighted
    est[OWN : OWN + 1, :] = jnp.sum(fst[...] * bias_sum, axis=0, keepdims=True)
    erx[e] = est[...]
    for k in (2, 1, 3):
        e_copy(k).start()
    received(erx.at[0:3], e_r)
    sum_ref[...] = (erx[0] + erx[1]) + (erx[2] + erx[3])

    sent(x_bytes(N_EX, 2), xh_s)
    sent(gp.at[:, 0:6], gh_s)
    sent(crx, c_s)
    sent(y1tx, y1_s)
    sent(y2tx, y2_s)
    sent(zst.at[0:7], z_s)
    sent(b1rx.at[0:7], b1_s)
    sent(b2rx.at[0:7], b2_s)
    sent(n1rx.at[0:7], n1_s)
    sent(n2rx.at[0:7], n2_s)
    sent(erx.at[0:3], e_s)


def finish(clip, scale, grad_ref, sum_ref, nw_ref, nb_ref, out_hbm, gw_hbm, gb_hbm, gw_ref, gb_ref, sems):
    stores = [pltpu.make_async_copy(grad_ref.at[n], out_hbm.at[n], sems.at[n]) for n in range(N_EX)]
    stores.append(pltpu.make_async_copy(gw_ref, gw_hbm, sems.at[N_EX]))
    stores.append(pltpu.make_async_copy(gb_ref, gb_hbm, sems.at[N_EX + 1]))
    for store in stores[:N_EX]:
        store.start()
    gw_ref[...] = (sum_ref[0:OWN] + noise_multiplier * clip * nw_ref[...]) * scale
    gb_ref[...] = (sum_ref[OWN : OWN + 1] + noise_multiplier * clip * nb_ref[...]) * scale
    for store in stores[N_EX:]:
        store.start()
    for store in stores:
        store.wait()


def local(inputs, cotangent, weight, bias, noise_weight, noise_bias):
    examples, tile_rows, tile_cols, channels = inputs.shape
    height = tile_rows * lax.axis_size("row")
    width = tile_cols * lax.axis_size("col")
    clip = math.sqrt(height * width * 9 * channels * channels)
    scale = 1.0 / math.sqrt(examples * lax.axis_size("ex") * height * width)
    vmem, hbm = pl.BlockSpec(memory_space=pltpu.VMEM), pl.BlockSpec(memory_space=pltpu.MemorySpace.HBM)
    halo_col, halo_cor = pltpu.VMEM((2, N_EX, TILE, CH), BF16), pltpu.VMEM((4, N_EX, 16, CH), BF16)
    spots = pltpu.VMEM((2, 4, N_EX, CH), F32)
    dma = pltpu.SemaphoreType.DMA
    input_grad, total = pl.pallas_call(
        functools.partial(kernel, clip),
        out_shape=(
            jax.ShapeDtypeStruct(inputs.shape, BF16),
            jax.ShapeDtypeStruct((24, channels), F32),
        ),
        in_specs=[hbm] * 4,
        out_specs=[vmem, vmem],
        scratch_shapes=[
            pltpu.VMEM((3, 3 * CH, CH), BF16),
            pltpu.VMEM((1, CH), F32),
            halo_col, spots,
            pltpu.VMEM((TILE * 16, CH), F32),
            pltpu.VMEM((N_EX, TILE + 2, TILE, CH), BF16),
            pltpu.VMEM((N_EX, TILE, TILE, CH), BF16),
            pltpu.VMEM((N_EX, TILE + 2, TILE, CH), BF16),
            halo_col, spots, halo_col, halo_cor, halo_col, halo_cor,
            pltpu.VMEM(((TILE + 2) * PITCH, CH), F32),
            pltpu.VMEM((2, TILE + 2, TILE, 3 * CH), BF16),
            pltpu.VMEM((CH, PIX), BF16),
            pltpu.VMEM((PIX, CH), F32),
            pltpu.VMEM((3, 3 * CH, CH), BF16),
            pltpu.VMEM((PIX, CH), F32),
            pltpu.VMEM((N_EX, 2, 4, CHUNK, CH), BF16),
            pltpu.VMEM((N_EX, 4, CHUNK, CH), BF16),
            pltpu.VMEM((N_EX, 2, CHUNK, CH), F32),
            pltpu.VMEM((N_EX, 2, CHUNK, CH), BF16),
            pltpu.VMEM((N_EX, 2, CHUNK, CH), BF16),
            pltpu.VMEM((N_EX, CHUNK, CH), F32),
            pltpu.VMEM((N_EX, CHUNK, CH), BF16),
            pltpu.VMEM((N_EX, CHUNK, CH), BF16),
            pltpu.VMEM((CHUNK + 16, CH), F32),
            pltpu.VMEM((8, N_EX, PIECE, CH), BF16),
            pltpu.VMEM((8, N_EX, PIECE, CH), BF16),
            pltpu.VMEM((N_EX, 24, CH), F32),
            pltpu.VMEM((N_EX, 8, CH), F32),
            pltpu.VMEM((N_EX, CH), F32),
            pltpu.VMEM((8, N_EX, CH), F32),
            pltpu.VMEM((N_EX, CH), F32),
            pltpu.VMEM((8, N_EX, CH), F32),
            pltpu.VMEM((1, CH), F32),
            pltpu.VMEM((8, 1, CH), F32),
            pltpu.VMEM((1, CH), F32),
            pltpu.VMEM((8, 1, CH), F32),
            pltpu.VMEM((N_EX, CH), F32),
            pltpu.VMEM((24, CH), F32),
            pltpu.VMEM((4, 24, CH), F32),
            dma((2,)), dma((N_EX,)), dma(()),
            dma(()), dma((2,)), dma(()), dma((N_EX,)),
            dma(()), dma((N_EX,)), dma(()), dma((N_EX,)), dma(()), dma((N_EX,)), dma(()), dma(()),
            dma(()), dma(()), dma(()), dma(()), dma(()), dma(()), dma(()), dma(()), dma(()), dma(()),
        ],
        compiler_params=pltpu.CompilerParams(
            collective_id=0, has_side_effects=True, vmem_limit_bytes=48 * 2**20
        ),
        name="clipped_grad",
    )(
        *(
            pltpu.with_memory_space_constraint(operand, pltpu.MemorySpace.HBM)
            for operand in (
                inputs, cotangent, weight.reshape(3, 3 * channels, channels), bias.reshape(1, channels)
            )
        )
    )
    input_grad, grad_weight, grad_bias = pl.pallas_call(
        functools.partial(finish, clip, scale),
        out_shape=(
            jax.ShapeDtypeStruct(inputs.shape, BF16),
            jax.ShapeDtypeStruct(noise_weight.shape, F32),
            jax.ShapeDtypeStruct((1, channels), F32),
        ),
        in_specs=[vmem] * 4,
        out_specs=[hbm] * 3,
        scratch_shapes=[
            pltpu.VMEM(noise_weight.shape, F32), pltpu.VMEM((1, channels), F32), dma((N_EX + 2,))
        ],
        compiler_params=pltpu.CompilerParams(vmem_limit_bytes=16 * 2**20),
        name="finish",
    )(input_grad, total, noise_weight, noise_bias.reshape(1, channels))
    return input_grad, grad_weight, grad_bias.reshape(channels)


def solution(mesh):
    in_specs = (
        P("ex", "row", "col", None),
        P("ex", "row", "col", None),
        P(),
        P(),
        P(("row", "col"), None),
        P(),
    )
    out_specs = (P("ex", "row", "col", None), P(("row", "col"), None), P())
    return jax.shard_map(local, mesh=mesh, in_specs=in_specs, out_specs=out_specs, check_vma=False)
```

```python
import functools
import math

import jax
import jax.numpy as jnp
from jax import lax
from jax.experimental import pallas as pl
from jax.experimental.pallas import tpu as pltpu
from jax.sharding import PartitionSpec as P

noise_multiplier = 0.002
epsilon = 1e-06
F32 = jnp.float32
BF16 = jnp.bfloat16
N_EX = 8
TILE = 32
CH = 128
PITCH = 48
PIX = TILE * TILE
ROWS = 9 * CH
CHUNK = ROWS // 8
EARLY = 1
OWN = CHUNK // 8
PIECE = 32


def kernel(
    clip,
    x_hbm, cot_hbm, w_hbm, b_hbm,
    out_ref, sum_ref,
    w_ref, b_ref, xe_ref, xc_ref, edge, xp, cot, gp, xcol, xcor, gcol, gcor, ge, gc, wide, taps, gt, g32, wback, acc,
    stage, crx, y1own, y1tx, y1rx, y2own, y2tx, y2rx, t32, zst, zrx, zacc, bpart,
    b1st, b1rx, b2st, b2rx, n1st, n1rx, n2st, n2rx, fst, est, erx,
    lw_s, lx_s, lc_s, xh_s, xh_r, gh_s, gh_r, c_s, c_r, y1_s, y1_r, y2_s, y2_r, z_s, z_r,
    b1_s, b1_r, b2_s, b2_r, n1_s, n1_r, n2_s, n2_r, e_s, e_r,
):
    e, r, c = lax.axis_index("ex"), lax.axis_index("row"), lax.axis_index("col")
    core, y = r % 2, r // 2
    up, down, left, right = (r + 7) % 8, (r + 1) % 8, (c + 7) % 8, (c + 1) % 8
    mate = r + 1 - 2 * core
    flip, mirror = y + 1 - 2 * (y % 2), 3 - y
    p1 = flip + core * (mirror - flip)
    p2 = mirror + core * (flip - mirror)
    far = (y + 2) % 4
    corners = ((up, left), (up, right), (down, left), (down, right))

    def remote(src, dst, s_sem, r_sem, to_row, to_col, to_ex=None):
        return pltpu.make_async_remote_copy(
            src_ref=src, dst_ref=dst, send_sem=s_sem, recv_sem=r_sem,
            device_id=(e if to_ex is None else to_ex, to_row, to_col),
            device_id_type=pl.DeviceIdType.MESH,
        )

    def received(view, sem):
        remote(view, view, sem, sem, r, c).wait_recv()

    def sent(view, sem):
        remote(view, view, sem, sem, r, c).wait_send()

    def load_x(n):
        return pltpu.make_async_copy(x_hbm.at[n], xp.at[n, 1 : TILE + 1], lx_s.at[n])

    barrier = pltpu.get_barrier_semaphore()
    partners = list(corners)
    partners += [((r + k) % 8, c) for k in range(1, 8)]
    partners += [(r, (c + k) % 8) for k in range(1, 8)]
    for to_row, to_col in partners:
        pl.semaphore_signal(barrier, inc=1, device_id=(e, to_row, to_col), device_id_type=pl.DeviceIdType.MESH)
    for k in range(1, 4):
        pl.semaphore_signal(barrier, inc=1, device_id=((e + k) % 4, r, c), device_id_type=pl.DeviceIdType.MESH)

    load_w = pltpu.make_async_copy(w_hbm, w_ref, lw_s.at[0])
    load_b = pltpu.make_async_copy(b_hbm, b_ref, lw_s.at[1])
    for n in range(N_EX):
        load_x(n).start()
    load_w.start()
    load_b.start()
    load_cot = pltpu.make_async_copy(cot_hbm, cot, lc_s)
    load_cot.start()

    pl.semaphore_wait(barrier, 21)

    batches = ((0, EARLY), (EARLY, N_EX))

    def x_rows(k):
        some = pl.ds(batches[k][0], batches[k][1] - batches[k][0])
        return [
            remote(x_hbm.at[some, TILE - 1], xp.at[some, 0], xh_s, xh_r.at[k], down, c),
            remote(x_hbm.at[some, 0], xp.at[some, TILE + 1], xh_s, xh_r.at[k], up, c),
        ]

    def x_columns(k):
        some = pl.ds(batches[k][0], batches[k][1] - batches[k][0])
        copies = [
            remote(xe_ref.at[1, some], xcol.at[0, some], xh_s, xh_r.at[k], r, right),
            remote(xe_ref.at[0, some], xcol.at[1, some], xh_s, xh_r.at[k], r, left),
        ]
        for i, (to_row, to_col) in enumerate(corners):
            copies.append(remote(xc_ref.at[k, i], xcor.at[k, 3 - i], xh_s, xh_r.at[k], to_row, to_col))
        return copies

    def x_bytes(examples, parts):
        return acc.at[0 : 2 * TILE * examples + 4 * N_EX * parts]

    def g_halo(n):
        copies = [
            remote(gp.at[n, TILE], gp.at[n, 0], gh_s, gh_r.at[n], down, c),
            remote(gp.at[n, 1], gp.at[n, TILE + 1], gh_s, gh_r.at[n], up, c),
            remote(ge.at[1, n], gcol.at[0, n], gh_s, gh_r.at[n], r, right),
            remote(ge.at[0, n], gcol.at[1, n], gh_s, gh_r.at[n], r, left),
        ]
        for k, (to_row, to_col) in enumerate(corners):
            copies.append(remote(gc.at[k, n], gcor.at[3 - k, n], gh_s, gh_r.at[n], to_row, to_col))
        return copies

    def clear(pad, col, cor, at, count):
        row_zero = jnp.zeros((count, 1, TILE, CH), BF16)
        col_zero = jnp.zeros((1, count, TILE, CH), BF16)
        cor_zero = jnp.zeros(cor.shape[1:], cor.dtype)

        @pl.when(r == 0)
        def _():
            pad[at, 0:1] = row_zero
            cor[0] = cor_zero
            cor[1] = cor_zero

        @pl.when(r == 7)
        def _():
            pad[at, TILE + 1 : TILE + 2] = row_zero
            cor[2] = cor_zero
            cor[3] = cor_zero

        @pl.when(c == 0)
        def _():
            col[0:1, at] = col_zero
            cor[0] = cor_zero
            cor[2] = cor_zero

        @pl.when(c == 7)
        def _():
            col[1:2, at] = col_zero
            cor[1] = cor_zero
            cor[3] = cor_zero

    def clear_x(k):
        begin, end = batches[k]
        clear(xp, xcol, xcor.at[k], pl.ds(begin, end - begin), end - begin)

    def spread(tap, pad, col, spot, n):
        tile = wide.reshape(TILE + 2, PITCH, CH)
        tile[:, 8 : 8 + TILE, :] = pad[n].astype(F32)
        for side, slot in ((0, 7), (1, 8 + TILE)):
            wide[pl.ds(PITCH + slot, TILE, stride=PITCH), :] = col[side, n].astype(F32)
            wide[slot : slot + 1, :] = spot(side)
            last = (TILE + 1) * PITCH + slot
            wide[last : last + 1, :] = spot(2 + side)
        tap[:, :, CH : 2 * CH] = pad[n]
        tap[:, :, 0:CH] = tile[:, 7 : 7 + TILE, :].astype(BF16)
        tap[:, :, 2 * CH :] = tile[:, 9 : 9 + TILE, :].astype(BF16)

    def conv(tap, weights):
        total = None
        for a in range(3):
            part = jnp.dot(
                tap[a : a + TILE].reshape(PIX, 3 * CH), weights[a], preferred_element_type=F32
            )
            total = part if total is None else total + part
        return total

    def core_copy(m):
        return remote(stage.at[m, 1 - core], crx.at[m], c_s, c_r.at[m], mate, c)

    def y1_copy(m):
        return remote(y1tx.at[m], y1rx.at[m], y1_s, y1_r.at[m], 2 * p1 + core, c)

    def y2_copy(m):
        return remote(y2tx.at[m], y2rx.at[m], y2_s, y2_r.at[m], 2 * p2 + core, c)

    def z_copy(m, k):
        to = (c + k) % 8
        return remote(zst.at[to, m], zrx.at[c, m], z_s, z_r, r, to)

    def step_y1(m):
        core_copy(m).wait_recv()

        def both(j):
            return stage[m, core, j].astype(F32) + crx[m, j].astype(F32)

        y1tx[m, 0] = both(p1).astype(BF16)
        y1tx[m, 1] = both(far).astype(BF16)
        y1_copy(m).start()
        y1own[m, 0] = both(y)
        y1own[m, 1] = both(p2)

    def step_y2(m):
        y1_copy(m).wait_recv()
        y2tx[m] = (y1own[m, 1] + y1rx[m, 1].astype(F32)).astype(BF16)
        y2_copy(m).start()
        y2own[m] = y1own[m, 0] + y1rx[m, 0].astype(F32)

    def step_z(m):
        y2_copy(m).wait_recv()
        t32[0:CHUNK, :] = y2own[m] + y2rx[m].astype(F32)
        for k in range(8):
            piece = t32[k * OWN : k * OWN + PIECE, :].astype(BF16)
            zst[k, m] = piece
        for k in (4, 3, 5, 2, 6, 1, 7):
            z_copy(m, k).start()
        zrx[c, m] = zst[c, m]

    for k in range(2):
        for copy in x_rows(k):
            copy.start()

    def take_edges(k, n):
        load_x(n).wait()
        for side in range(2):
            block = xp[n, 1 : TILE + 1, side * 16 : side * 16 + 16, :].astype(F32)
            edge[...] = block.reshape(TILE * 16, CH)
            column = edge[pl.ds(15 * side, TILE, stride=16), :]
            xe_ref[side, n] = column.astype(BF16)
            xc_ref[k, side, pl.ds(n, 1), :] = column[0:1]
            xc_ref[k, 2 + side, pl.ds(n, 1), :] = column[TILE - 1 : TILE]

    xc_ref[...] = jnp.zeros_like(xc_ref)
    for k, (begin, end) in enumerate(batches):
        lax.fori_loop(begin, end, lambda n, carry, k=k: (take_edges(k, n), carry)[1], 0)
        for copy in x_columns(k):
            copy.start()
    load_w.wait()
    load_b.wait()
    for a in range(3):
        for b in range(3):
            wback[2 - a, (2 - b) * CH : (3 - b) * CH, :] = w_ref[a, b * CH : (b + 1) * CH, :].T
    t32[...] = jnp.zeros_like(t32)
    load_cot.wait()
    received(x_bytes(EARLY, 1), xh_r.at[0])
    clear_x(0)

    def forward(n):
        tap = taps.at[n % 2]
        batch = 0 if isinstance(n, int) else (n + N_EX - EARLY) // N_EX
        spread(tap, xp, xcol, lambda k: xcor[batch, k, pl.ds(n, 1), :], n)
        acc[...] = conv(tap, w_ref)

    def output_grad(n):
        half = 0.5 * (acc[...] + b_ref[...])
        t = jnp.tanh(half)
        slope = (1.0 + t) + half * (1.0 - t * t)
        g = (0.5 * cot[n].reshape(PIX, CH).astype(F32) * slope).astype(BF16)
        gp[n, 1 : TILE + 1] = g.reshape(TILE, TILE, CH)
        wide_g = g.astype(F32)
        g32[...] = wide_g
        bpart[n] = jnp.sum(wide_g.reshape(PIX // 8, 8, CH), axis=0)
        ge[0, n] = g32[pl.ds(0, TILE, stride=TILE), :].astype(BF16)
        ge[1, n] = g32[pl.ds(TILE - 1, TILE, stride=TILE), :].astype(BF16)
        for k, at in enumerate((0, TILE - 1, PIX - TILE, PIX - 1)):
            gc[k, n] = jnp.broadcast_to(g32[at : at + 1, :], (16, CH)).astype(BF16)

    def transpose_grad(n):
        gt[...] = gp[n, 1 : TILE + 1].reshape(PIX, CH).T

    def kernel_grad(n):
        tap = taps.at[n % 2]
        every = jnp.concatenate(
            [tap[a : a + TILE].reshape(PIX, 3 * CH) for a in range(3)], axis=1
        )
        for start in range(0, ROWS, 2 * CH):
            part = jnp.dot(gt[...], every[:, start : start + 2 * CH], preferred_element_type=F32)
            for b in range(part.shape[1] // CH):
                block = part[:, b * CH : (b + 1) * CH].T.astype(BF16)
                for k in range(8):
                    group = start // 16 + 8 * b + k
                    owner, at = group // 9, group % 9 * 16
                    stage[n, owner % 2, owner // 2, at : at + 16, :] = block[16 * k : 16 * k + 16]

    def first(n, carry):
        @pl.when(n == EARLY)
        def _():
            received(x_bytes(N_EX - EARLY, 1), xh_r.at[1])
            clear_x(1)

        forward(n)
        kernel_grad(n - 1)
        output_grad(n)
        transpose_grad(n)
        for copy in g_halo(n):
            copy.start()
        core_copy(n - 1).start()

        @pl.when(n >= 2)
        def _():
            step_y1(n - 2)

        @pl.when(n >= 4)
        def _():
            step_y2(n - 4)

        @pl.when(n >= 6)
        def _():
            step_z(n - 6)

        return carry

    forward(0)
    output_grad(0)
    transpose_grad(0)
    for copy in g_halo(0):
        copy.start()
    lax.fori_loop(1, N_EX, first, 0)
    kernel_grad(N_EX - 1)
    core_copy(N_EX - 1).start()

    def b1_copy(k):
        return remote(b1st, b1rx.at[c], b1_s, b1_r, r, (c + k) % 8)

    def b2_copy(k):
        return remote(b2st, b2rx.at[r], b2_s, b2_r, (r + k) % 8, c)

    def n1_copy(k):
        return remote(n1st, n1rx.at[c], n1_s, n1_r, r, (c + k) % 8)

    def n2_copy(k):
        return remote(n2st, n2rx.at[r], n2_s, n2_r, (r + k) % 8, c)

    def e_copy(k):
        return remote(est, erx.at[e], e_s, e_r, r, c, (e + k) % 4)

    away = (4, 3, 5, 2, 6, 1, 7)

    def add_up(rx):
        total = rx[0]
        for k in range(1, 8):
            total = total + rx[k]
        return total

    def bias_z(_):
        for m in range(N_EX):
            b1st[m : m + 1, :] = jnp.sum(bpart[m], axis=0, keepdims=True)
        b1rx[c] = b1st[...]
        for k in away:
            b1_copy(k).start()

    def bias_row(_):
        received(b1rx.at[0:7], b1_r)
        total = add_up(b1rx)
        b2st[...] = total
        b2rx[r] = total
        for k in away:
            b2_copy(k).start()

    plan = {
        0: ((step_z, 2), (step_y2, 4), (step_y1, 6), (bias_z, 0),),
        1: ((step_y1, 7), (step_z, 3),),
        2: ((step_y2, 5),),
        3: ((step_y2, 6), (step_z, 4),),
        4: ((step_y2, 7),),
        5: ((step_z, 5),),
        6: ((step_z, 6),),
        7: ((step_z, 7), (bias_row, 0),),
    }

    def second(n, carry):
        received(gp.at[n, 0:6], gh_r.at[n])
        clear(gp, gcol, gcor.at[:, n], pl.ds(n, 1), 1)
        spread(taps.at[0], gp, gcol, lambda k: gcor[k, n].astype(F32)[0:1], n)
        out_ref[n] = conv(taps.at[0], wback).astype(BF16).reshape(TILE, TILE, CH)
        for when, steps in plan.items():

            @pl.when(n == when)
            def _(steps=steps):
                for step, m in steps:
                    step(m)

        return carry

    lax.fori_loop(0, N_EX, second, 0)

    keep = lax.broadcasted_iota(jnp.int32, (8, CH), 0) < OWN - 16
    own_lane = lax.broadcasted_iota(jnp.int32, (8, CH), 1) // 16 == lax.broadcasted_iota(jnp.int32, (8, CH), 0)
    received(zrx.at[0:7], z_r)
    for m in range(N_EX):
        total = zrx[0, m].astype(F32)
        for k in range(1, 8):
            total = total + zrx[k, m].astype(F32)
        zacc[m] = total[0:24]
        square = total * total
        part = square[0:8] + square[8:16] + jnp.where(keep, square[16:24], 0.0)
        fst[m : m + 1, :] = jnp.sum(part, axis=0, keepdims=True)
    folded = fst[...]
    for width in (64, 32, 16):
        folded = folded + pltpu.roll(folded, width, 1)
    total = jnp.sum(jnp.where(own_lane, folded, 0.0), axis=0, keepdims=True)
    n1st[...] = total
    n1rx[c] = total
    for k in away:
        n1_copy(k).start()
    received(b2rx.at[0:7], b2_r)
    bias_sum = add_up(b2rx)
    received(n1rx.at[0:7], n1_r)
    total = add_up(n1rx)
    n2st[...] = total
    n2rx[r] = total
    for k in away:
        n2_copy(k).start()
    received(n2rx.at[0:7], n2_r)
    total = add_up(n2rx)
    squares = jnp.where(own_lane, jnp.broadcast_to(total, (N_EX, CH)), 0.0) + bias_sum * bias_sum
    factor = jnp.minimum(1.0, clip / jnp.sqrt(jnp.sum(squares, axis=1, keepdims=True) + epsilon))
    fst[...] = jnp.broadcast_to(factor, (N_EX, CH))
    weighted = fst[0:1, :] * zacc[0]
    for m in range(1, N_EX):
        weighted = weighted + fst[m : m + 1, :] * zacc[m]
    est[...] = weighted
    est[OWN : OWN + 1, :] = jnp.sum(fst[...] * bias_sum, axis=0, keepdims=True)
    erx[e] = est[...]
    for k in (2, 1, 3):
        e_copy(k).start()
    received(erx.at[0:3], e_r)
    sum_ref[...] = (erx[0] + erx[1]) + (erx[2] + erx[3])

    sent(x_bytes(N_EX, 2), xh_s)
    sent(gp.at[:, 0:6], gh_s)
    sent(crx, c_s)
    sent(y1tx, y1_s)
    sent(y2tx, y2_s)
    sent(zst.at[0:7], z_s)
    sent(b1rx.at[0:7], b1_s)
    sent(b2rx.at[0:7], b2_s)
    sent(n1rx.at[0:7], n1_s)
    sent(n2rx.at[0:7], n2_s)
    sent(erx.at[0:3], e_s)


def finish(clip, scale, grad_ref, sum_ref, nw_ref, nb_ref, out_hbm, gw_hbm, gb_hbm, gw_ref, gb_ref, sems):
    stores = [pltpu.make_async_copy(grad_ref.at[n], out_hbm.at[n], sems.at[n]) for n in range(N_EX)]
    stores.append(pltpu.make_async_copy(gw_ref, gw_hbm, sems.at[N_EX]))
    stores.append(pltpu.make_async_copy(gb_ref, gb_hbm, sems.at[N_EX + 1]))
    for store in stores[:N_EX]:
        store.start()
    gw_ref[...] = (sum_ref[0:OWN] + noise_multiplier * clip * nw_ref[...]) * scale
    gb_ref[...] = (sum_ref[OWN : OWN + 1] + noise_multiplier * clip * nb_ref[...]) * scale
    for store in stores[N_EX:]:
        store.start()
    for store in stores:
        store.wait()


def local(inputs, cotangent, weight, bias, noise_weight, noise_bias):
    examples, tile_rows, tile_cols, channels = inputs.shape
    height = tile_rows * lax.axis_size("row")
    width = tile_cols * lax.axis_size("col")
    clip = math.sqrt(height * width * 9 * channels * channels)
    scale = 1.0 / math.sqrt(examples * lax.axis_size("ex") * height * width)
    vmem, hbm = pl.BlockSpec(memory_space=pltpu.VMEM), pl.BlockSpec(memory_space=pltpu.MemorySpace.HBM)
    halo_col, halo_cor = pltpu.VMEM((2, N_EX, TILE, CH), BF16), pltpu.VMEM((4, N_EX, 16, CH), BF16)
    spots = pltpu.VMEM((2, 4, N_EX, CH), F32)
    dma = pltpu.SemaphoreType.DMA
    input_grad, total = pl.pallas_call(
        functools.partial(kernel, clip),
        out_shape=(
            jax.ShapeDtypeStruct(inputs.shape, BF16),
            jax.ShapeDtypeStruct((24, channels), F32),
        ),
        in_specs=[hbm] * 4,
        out_specs=[vmem, vmem],
        scratch_shapes=[
            pltpu.VMEM((3, 3 * CH, CH), BF16),
            pltpu.VMEM((1, CH), F32),
            halo_col, spots,
            pltpu.VMEM((TILE * 16, CH), F32),
            pltpu.VMEM((N_EX, TILE + 2, TILE, CH), BF16),
            pltpu.VMEM((N_EX, TILE, TILE, CH), BF16),
            pltpu.VMEM((N_EX, TILE + 2, TILE, CH), BF16),
            halo_col, spots, halo_col, halo_cor, halo_col, halo_cor,
            pltpu.VMEM(((TILE + 2) * PITCH, CH), F32),
            pltpu.VMEM((2, TILE + 2, TILE, 3 * CH), BF16),
            pltpu.VMEM((CH, PIX), BF16),
            pltpu.VMEM((PIX, CH), F32),
            pltpu.VMEM((3, 3 * CH, CH), BF16),
            pltpu.VMEM((PIX, CH), F32),
            pltpu.VMEM((N_EX, 2, 4, CHUNK, CH), BF16),
            pltpu.VMEM((N_EX, 4, CHUNK, CH), BF16),
            pltpu.VMEM((N_EX, 2, CHUNK, CH), F32),
            pltpu.VMEM((N_EX, 2, CHUNK, CH), BF16),
            pltpu.VMEM((N_EX, 2, CHUNK, CH), BF16),
            pltpu.VMEM((N_EX, CHUNK, CH), F32),
            pltpu.VMEM((N_EX, CHUNK, CH), BF16),
            pltpu.VMEM((N_EX, CHUNK, CH), BF16),
            pltpu.VMEM((CHUNK + 16, CH), F32),
            pltpu.VMEM((8, N_EX, PIECE, CH), BF16),
            pltpu.VMEM((8, N_EX, PIECE, CH), BF16),
            pltpu.VMEM((N_EX, 24, CH), F32),
            pltpu.VMEM((N_EX, 8, CH), F32),
            pltpu.VMEM((N_EX, CH), F32),
            pltpu.VMEM((8, N_EX, CH), F32),
            pltpu.VMEM((N_EX, CH), F32),
            pltpu.VMEM((8, N_EX, CH), F32),
            pltpu.VMEM((1, CH), F32),
            pltpu.VMEM((8, 1, CH), F32),
            pltpu.VMEM((1, CH), F32),
            pltpu.VMEM((8, 1, CH), F32),
            pltpu.VMEM((N_EX, CH), F32),
            pltpu.VMEM((24, CH), F32),
            pltpu.VMEM((4, 24, CH), F32),
            dma((2,)), dma((N_EX,)), dma(()),
            dma(()), dma((2,)), dma(()), dma((N_EX,)),
            dma(()), dma((N_EX,)), dma(()), dma((N_EX,)), dma(()), dma((N_EX,)), dma(()), dma(()),
            dma(()), dma(()), dma(()), dma(()), dma(()), dma(()), dma(()), dma(()), dma(()), dma(()),
        ],
        compiler_params=pltpu.CompilerParams(
            collective_id=0, has_side_effects=True, vmem_limit_bytes=48 * 2**20
        ),
        name="clipped_grad",
    )(
        *(
            pltpu.with_memory_space_constraint(operand, pltpu.MemorySpace.HBM)
            for operand in (
                inputs, cotangent, weight.reshape(3, 3 * channels, channels), bias.reshape(1, channels)
            )
        )
    )
    input_grad, grad_weight, grad_bias = pl.pallas_call(
        functools.partial(finish, clip, scale),
        out_shape=(
            jax.ShapeDtypeStruct(inputs.shape, BF16),
            jax.ShapeDtypeStruct(noise_weight.shape, F32),
            jax.ShapeDtypeStruct((1, channels), F32),
        ),
        in_specs=[vmem] * 4,
        out_specs=[hbm] * 3,
        scratch_shapes=[
            pltpu.VMEM(noise_weight.shape, F32), pltpu.VMEM((1, channels), F32), dma((N_EX + 2,))
        ],
        compiler_params=pltpu.CompilerParams(vmem_limit_bytes=16 * 2**20),
        name="finish",
    )(input_grad, total, noise_weight, noise_bias.reshape(1, channels))
    return input_grad, grad_weight, grad_bias.reshape(channels)


def solution(mesh):
    in_specs = (
        P("ex", "row", "col", None),
        P("ex", "row", "col", None),
        P(),
        P(),
        P(("row", "col"), None),
        P(),
    )
    out_specs = (P("ex", "row", "col", None), P(("row", "col"), None), P())
    return jax.shard_map(local, mesh=mesh, in_specs=in_specs, out_specs=out_specs, check_vma=False)
```
